128 devices in a mesh: grp: 4 (over x), sub: 32 (over z, y, core).
Axes of the slice: x: 4, y: 4, z: 4, core: 2. Of those that a mesh axis runs over, the one named last changes fastest.
Arguments:
- vectors: bfloat16 [128, 262144], P(None, ('grp', 'sub')), may hold values from -6 to 6
- geometry: bfloat16 [4, 262144], P(None, ('grp', 'sub')), may hold values from 0 to 4, as said below
- transfer: float32 [2, 4, 4, 512], P(None, 'grp'), may hold values from -6 to 6
Outputs:
- ortho_basis: float32 [128, 262144], P(None, ('grp', 'sub'))
- r_factor: float32 [128, 128], replicated
The draws below stay inside these ranges and needn't reach their ends.
Inputs may be any that keep to these rules, and one draw needn't show every extreme that they name: `geometry`: rows 0 to 2 lie in the unit box, row 3 is positive and at least 0.25.
All inputs are finite; a program needn't handle non-finite values.
Results may differ from the reference program's by a relative error of at most 0.0065.
Values may be sent and summed in bfloat16 or wider, within the bound.
A program may use at most 128 MiB of HBM per device.

```python
import math
import jax
import jax.numpy as jnp
from jax import lax

VEC = 64
K = 512
P_SIZE = 2048
COLS = 128
NTOT = 262144
N_GRP = 4
N_SUB = 32


def draw_geometry(key, part):
    key_points = jax.random.fold_in(key, 11)
    key_weights = jax.random.fold_in(key, 12)
    points = jax.random.uniform(key_points, (3, NTOT), jnp.float32)
    lowest, highest = (0.5, 2.0)
    weights = jnp.exp(jax.random.uniform(key_weights, (1, NTOT), jnp.float32, math.log(lowest), math.log(highest)))
    return jnp.concatenate((points, weights), 0).astype(jnp.bfloat16)


def steps_of(stream_key, extent, shards, low, high):
    def one(dim, shards_of):
        steps = jax.random.uniform(jax.random.fold_in(jax.random.fold_in(stream_key, 6), dim), (shards_of,), jnp.float32, low / len(shards), high / len(shards))
        return jnp.repeat(jnp.exp(steps), extent[dim] // shards_of).reshape((-1,) + (1,) * (len(extent) - dim - 1))

    gain = one(*shards[0])
    for cut in shards[1:]:
        gain = gain * one(*cut)
    return gain


def gaussian(own_key, dims, scale, bound, cuts=(), dtype=jnp.bfloat16):
    array = jax.random.normal(own_key, dims, jnp.float32) * scale
    if len(cuts) > 0:
        array = steps_of(own_key, dims, cuts, -0.22, 0.18) * array
    return jnp.clip(array, min=-bound, max=bound).astype(dtype)


def setup_inputs(seed: int = 0) -> dict:
    arg_keys = jax.random.split(jax.random.key(seed), 4)
    vectors = gaussian(arg_keys[0], (COLS, NTOT), 1.0, 6.0, ((1, 128),))
    geometry = draw_geometry(jax.random.fold_in(arg_keys[3], 71), 0)
    transfer = gaussian(arg_keys[2], (2, N_GRP, N_GRP, K), 1.0, 6.0, ((1, 4),), jnp.float32)
    return {"vectors": vectors, "geometry": geometry, "transfer": transfer}


KWAVE = 20.0
DELTA = 0.25
GOLDEN = math.pi * (3.0 - math.sqrt(5.0))

def kernel_tables(target, source, offsets):
    target_f = target.astype(jnp.float32)
    source_f = source.astype(jnp.float32)
    diff_x = target_f[0][None, :] - source_f[0][:, None] - offsets[:, None]
    diff_y = target_f[1][None, :] - source_f[1][:, None]
    diff_z = target_f[2][None, :] - source_f[2][:, None]
    dist_sq = diff_x * diff_x + diff_y * diff_y + diff_z * diff_z
    spread = source_f[3][:, None] / jnp.sqrt(dist_sq + DELTA * DELTA)
    phases = KWAVE * jnp.sqrt(dist_sq)
    return ((spread * jnp.cos(phases)).astype(jnp.bfloat16), (spread * jnp.sin(phases)).astype(jnp.bfloat16))

def near_field(source_vec, source_geo, offsets, target_geo):
    half_cols = source_vec.shape[0] // 2
    panel_count = target_geo.shape[1]
    block_cols = min(512, panel_count)
    pieces = []
    for column in range(0, panel_count, block_cols):
        real_k, imag_k = kernel_tables(target_geo[:, column:column + block_cols], source_geo, offsets)
        part_a = jnp.dot(source_vec.astype(jnp.float32), real_k.astype(jnp.float32), preferred_element_type=jnp.float32)
        part_b = jnp.dot(source_vec.astype(jnp.float32), imag_k.astype(jnp.float32), preferred_element_type=jnp.float32)
        pieces.append(jnp.concatenate((part_a[:half_cols] - part_b[half_cols:], part_a[half_cols:] + part_b[:half_cols]), 0))
    return jnp.concatenate(pieces, 1)

def directions(dir_count):
    serial = jnp.arange(dir_count).astype(jnp.float32)
    height = 1.0 - (2.0 * serial + 1.0) / dir_count
    radius = jnp.sqrt(jnp.maximum(1.0 - height * height, 0.0))
    azimuth = serial * GOLDEN
    return (radius * jnp.cos(azimuth), radius * jnp.sin(azimuth), height)

def far_tables(geo, dir_count):
    points = geo.astype(jnp.float32)
    dir_x, dir_y, dir_z = directions(dir_count)
    phases = KWAVE * (dir_x[:, None] * points[0][None, :] + dir_y[:, None] * points[1][None, :] + dir_z[:, None] * points[2][None, :])
    cos_table = jnp.cos(phases)
    sin_table = jnp.sin(phases)
    weight = points[3][None, :]
    return ((weight * cos_table).astype(jnp.bfloat16), (weight * sin_table).astype(jnp.bfloat16), cos_table.astype(jnp.bfloat16), sin_table.astype(jnp.bfloat16))

def reference(vectors, geometry, transfer):
    dev_count = N_GRP * N_SUB
    vec_dev = vectors.reshape(COLS, dev_count, P_SIZE).transpose(1, 0, 2)
    geo_dev = geometry.reshape(4, dev_count, P_SIZE).transpose(1, 0, 2)
    vec_grid = vec_dev.reshape(N_GRP, N_SUB, COLS, P_SIZE)
    geo_grid = geo_dev.reshape(N_GRP, N_SUB, 4, P_SIZE)
    zero_vec = jnp.zeros((N_GRP, 1, COLS, P_SIZE), jnp.bfloat16)
    zero_geo = jnp.zeros((N_GRP, 1, 4, P_SIZE), jnp.bfloat16)
    ext_vec = jnp.concatenate((jnp.concatenate((zero_vec, vec_grid[:, :-1]), 1), vec_grid, jnp.concatenate((vec_grid[:, 1:], zero_vec), 1)), 3).reshape(dev_count, COLS, 3 * P_SIZE)
    ext_geo = jnp.concatenate((jnp.concatenate((zero_geo, geo_grid[:, :-1]), 1), geo_grid, jnp.concatenate((geo_grid[:, 1:], zero_geo), 1)), 3).reshape(dev_count, 4, 3 * P_SIZE)
    offsets = jnp.concatenate((-jnp.ones((P_SIZE,), jnp.float32), jnp.zeros((P_SIZE,), jnp.float32), jnp.ones((P_SIZE,), jnp.float32)))

    def near_device(device_item):
        return near_field(device_item[0], device_item[1], offsets, device_item[2])
    near_all = lax.map(near_device, (ext_vec, ext_geo, geo_dev))
    moment_scale = (P_SIZE * N_SUB) ** (-0.5)
    near_scale = (3 * P_SIZE) ** (-0.5)
    far_scale = (K * N_GRP) ** (-0.5)

    def device_moment(device_item):
        src_cos, src_sin, eval_cos, eval_sin = far_tables(device_item[1], K)
        part_x = jnp.dot(device_item[0].astype(jnp.float32), src_cos.T.astype(jnp.float32), preferred_element_type=jnp.float32)
        part_z = jnp.dot(device_item[0].astype(jnp.float32), src_sin.T.astype(jnp.float32), preferred_element_type=jnp.float32)
        return jnp.concatenate((part_x[:VEC] + part_z[VEC:], part_x[VEC:] - part_z[:VEC]), 0) * moment_scale
    moments = lax.map(device_moment, (vec_dev, geo_dev))
    group_sum = lax.optimization_barrier(jnp.sum(moments.reshape(N_GRP, N_SUB, COLS, K), axis=1))
    tran_re = transfer[0][:, :, None, :]
    tran_im = transfer[1][:, :, None, :]
    mom_re = group_sum[None, :, :VEC, :]
    mom_im = group_sum[None, :, VEC:, :]
    local_re = lax.optimization_barrier(jnp.sum(tran_re * mom_re - tran_im * mom_im, axis=1))
    local_im = lax.optimization_barrier(jnp.sum(tran_re * mom_im + tran_im * mom_re, axis=1))
    local_exp = jnp.concatenate((local_re, local_im), 1).astype(jnp.bfloat16)
    local_dev = jnp.repeat(local_exp, N_SUB, axis=0)

    def device_apply(device_item):
        vec_here, geo_here, local_here, near_here = device_item
        src_cos, src_sin, eval_cos, eval_sin = far_tables(geo_here, K)
        part_a = jnp.dot(local_here.astype(jnp.float32), eval_cos.astype(jnp.float32), preferred_element_type=jnp.float32)
        part_b = jnp.dot(local_here.astype(jnp.float32), eval_sin.astype(jnp.float32), preferred_element_type=jnp.float32)
        far_part = jnp.concatenate((part_a[:VEC] - part_b[VEC:], part_a[VEC:] + part_b[:VEC]), 0)
        total = 0.5 * vec_here.astype(jnp.float32) + near_scale * near_here + far_scale * far_part
        return total.astype(jnp.bfloat16)
    applied = lax.map(device_apply, (vec_dev, geo_dev, local_dev, near_all))
    applied_f = applied.astype(jnp.float32)
    gram_mat = jnp.einsum('dcp,dep->ce', applied_f, applied_f, precision=lax.Precision.HIGHEST) * (1.0 / NTOT)
    lower_fac = jnp.linalg.cholesky(gram_mat)
    applied_flat = applied_f.transpose(1, 0, 2).reshape(COLS, NTOT)
    ortho_basis = lax.linalg.triangular_solve(lower_fac, applied_flat, left_side=True, lower=True)
    return (ortho_basis, lower_fac.T)
```

```python
import functools
import math

import jax
import jax.numpy as jnp
import numpy as np
from jax import lax
from jax.experimental import pallas as pl
from jax.experimental.pallas import tpu as pltpu
from jax.sharding import PartitionSpec as P

F32 = jnp.float32
BF16 = jnp.bfloat16
MESH = pl.DeviceIdType.MESH

KWAVE = 20.0
DELTA = 0.25
GOLDEN = math.pi * (3.0 - math.sqrt(5.0))
TURN = KWAVE / (2.0 * math.pi)
SOFT = DELTA * DELTA * TURN * TURN
Q0 = -1.03910273
P0, P1, P2 = -0.33076115, 1.40669993, -0.3346358
MAGIC = 1.5 * 2.0**23

TILE = 512
ROWS = 64
NT = (((1,), (1,)), ((), ()))
TN = (((0,), (0,)), ((), ()))


def half_angle(t):
    f = t - ((t + MAGIC) - MAGIC)
    u = f * f
    return (P2 * u + P1) * u + P0, f * (u + Q0)


def rotated(x, axis):
    half = x.shape[axis] // 2
    re = lax.slice_in_dim(x, 0, half, axis=axis)
    im = lax.slice_in_dim(x, half, 2 * half, axis=axis)
    return jnp.concatenate((-im, re), axis)


def lane_rotated(x):
    half = x.shape[-1] // 2
    lane = lax.broadcasted_iota(jnp.int32, x.shape, x.ndim - 1)
    turned = pltpu.roll(x, half, x.ndim - 1)
    return jnp.where(lane < half, -turned, turned)


def remote(src, dst, send_sem, recv_sem, device):
    return pltpu.make_async_remote_copy(
        src_ref=src,
        dst_ref=dst,
        send_sem=send_sem,
        recv_sem=recv_sem,
        device_id=device,
        device_id_type=MESH,
    )


def product_kernel(
    n_grp, n_sub,
    vec, geo, tran, dirs, sel,
    applied, gram,
    wv, wv_nb, geo_nb, tables, moment, mom_recv, grp_src, grp_recv, tran_t, loc, loc_mat,
    xrep, yrep, w2, g, acc, q, z_send, z_recv,
    gram_src, gram_recv, gsum_recv, gram_all,
    halo_s, halo_r, mom_s, mom_r, grp_s, grp_r, loc_s, loc_r, z_s, z_r,
    gr_s, gr_r, gg_s, gg_r, ga_s, ga_r,
):
    cols, panels = vec.shape
    dir_count = dirs.shape[0]
    chunk = dir_count // n_sub
    n_tiles = panels // TILE
    me_s = lax.axis_index("sub")
    me_g = lax.axis_index("grp")
    has_right = me_s < n_sub - 1
    has_left = me_s > 0

    def peer(k):
        return lax.rem(me_s + k, n_sub)

    def peer_g(k):
        return lax.rem(me_g + k, n_grp)

    barrier = pltpu.get_barrier_semaphore()

    def greet(k, _):
        pl.semaphore_signal(barrier, inc=1, device_id={"sub": peer(k)}, device_id_type=MESH)
        return 0

    lax.fori_loop(1, n_sub, greet, 0)

    def greet_g(k, _):
        pl.semaphore_signal(barrier, inc=1, device_id={"grp": peer_g(k)}, device_id_type=MESH)
        return 0

    lax.fori_loop(1, n_grp, greet_g, 0)

    weight = geo[3:4, :].astype(F32)
    wv[...] = (vec[...].astype(F32) * weight).astype(BF16)

    pl.semaphore_wait(barrier, n_sub - 1 + n_grp - 1)

    def halo(dst_sub):
        return (
            remote(wv, wv_nb, halo_s.at[0], halo_r.at[0], {"sub": dst_sub}),
            remote(geo, geo_nb, halo_s.at[1], halo_r.at[1], {"sub": dst_sub}),
        )

    left = lax.rem(me_s + n_sub - 1, n_sub)
    right = lax.rem(me_s + 1, n_sub)

    @pl.when(has_left)
    def _():
        for copy in halo(left):
            copy.start()

    def far_tables(n, _):
        k = n // n_tiles
        col = pl.multiple_of((n % n_tiles) * TILE, TILE)
        turns = jnp.dot(
            dirs[pl.ds(pl.multiple_of(k * 128, 128), 128), :],
            geo[:, pl.ds(col, TILE)],
            preferred_element_type=F32,
        )
        a, b = half_angle(turns)
        aa, bb = a * a, b * b
        norm = aa + bb
        inv = lax.rsqrt(norm * norm)
        row = pl.multiple_of(k * 256, 256)
        tables[pl.ds(row, 128), pl.ds(col, TILE)] = ((aa - bb) * inv).astype(BF16)
        tables[pl.ds(row + 128, 128), pl.ds(col, TILE)] = (a * b * inv).astype(BF16)
        return 0

    lax.fori_loop(0, dir_count // 128 * n_tiles, far_tables, 0)

    moment_scale = (panels * n_sub) ** (-0.5)
    for k in range(dir_count // 128):
        both = lax.dot_general(
            tables[k * 256 : k * 256 + 256, :], wv[...], NT, preferred_element_type=F32
        )
        moment[k * 128 : k * 128 + 128, :] = (
            both[:128] - 2.0 * lane_rotated(both[128:])
        ) * moment_scale

    def rows_of(ref, i, size):
        return ref.at[pl.ds(pl.multiple_of(i * size, size), size), :]

    def send_moment(k, _):
        p = peer(k)
        remote(
            rows_of(moment, p, chunk), mom_recv.at[me_s], mom_s.at[p], mom_r.at[me_s], {"sub": p}
        ).start()
        return 0

    lax.fori_loop(1, n_sub, send_moment, 0)

    for k in range(3):
        xrep[k] = jnp.broadcast_to(geo[k : k + 1, :].astype(F32) * TURN, (8, panels))

    def source_side(geo_ref, wv_ref, base, offset):
        for k in range(3):
            def spread(n, _):
                col = pl.multiple_of(n * TILE, TILE)
                y = lax.dot_general(
                    geo_ref[:, pl.ds(col, TILE)], sel[:, k * 128 : k * 128 + 128], TN,
                    preferred_element_type=F32,
                )
                if k == 0 and offset:
                    y = y + float(offset)
                yrep[k, pl.ds(base + col, TILE), :] = y * TURN
                return 0
            lax.fori_loop(0, n_tiles, spread, 0)
        for n in range(panels // 128):
            block = wv_ref[:, n * 128 : n * 128 + 128].astype(F32)
            at = 2 * base + n * 256
            w2[:, at : at + 128] = block.astype(BF16)
            w2[:, at + 128 : at + 256] = (2.0 * rotated(block, 0)).astype(BF16)

    source_side(geo, wv, 0, 0)
    acc[...] = jnp.zeros_like(acc)

    def near_tile(source, target, symmetric):
        i0 = pl.multiple_of(target * TILE, TILE)

        def strip(r, _):
            for l in range(0, TILE, 128):
                for sub in range(0, ROWS, 16):
                    row = pl.multiple_of(source * TILE + r * ROWS, ROWS) + sub

                    def diff(k):
                        y = yrep[k, pl.ds(row, 16), :].reshape(2, 8, 128)
                        return xrep[k, :, pl.ds(pl.multiple_of(i0 + l, 128), 128)] - y

                    dx, dy, dz = diff(0), diff(1), diff(2)
                    d2 = dx * dx + dy * dy + dz * dz
                    d2e = d2 + 1e-30
                    a, b = half_angle(d2e * lax.rsqrt(d2e))
                    aa, bb = a * a, b * b
                    norm = aa + bb
                    inv = lax.rsqrt(norm * norm * (d2 + SOFT))
                    at = pl.multiple_of(
                        (r * ROWS) // 128 * 256 + lax.rem(r * ROWS, 128), ROWS
                    ) + sub
                    g[pl.ds(at, 16), l : l + 128] = (
                        ((aa - bb) * inv).reshape(16, 128).astype(BF16)
                    )
                    g[pl.ds(at + 128, 16), l : l + 128] = (
                        ((a * b) * inv).reshape(16, 128).astype(BF16)
                    )
            return 0

        lax.fori_loop(0, TILE // ROWS, strip, 0)
        acc[:, pl.ds(i0, TILE)] += jnp.dot(
            w2[:, pl.ds(pl.multiple_of(source * 2 * TILE, 2 * TILE), 2 * TILE)],
            g[...],
            preferred_element_type=F32,
        )
        if symmetric:
            q[...] += lax.dot_general(
                wv[:, pl.ds(i0, TILE)], g[...], NT, preferred_element_type=F32
            )

    def mirrored(n):
        re = q[:, n * 256 : n * 256 + 128]
        im = q[:, n * 256 + 128 : n * 256 + 256]
        return re + 2.0 * rotated(im, 0)

    def send_z(j):
        return remote(z_send.at[j], z_recv.at[j], z_s.at[j], z_r.at[j], {"sub": right})

    @pl.when(has_right)
    def _():
        for copy in halo(left):
            copy.wait_recv()
        source_side(geo_nb, wv_nb, panels, 1)

    def neighbour_block(j):
        @pl.when(has_right)
        def _():
            q[...] = jnp.zeros_like(q)

            def step(i, _):
                near_tile(n_tiles + j, i, True)
                return 0

            lax.fori_loop(0, n_tiles, step, 0)
            for n in range(TILE // 128):
                z_send[j, :, n * 128 : n * 128 + 128] = mirrored(n).astype(BF16)
            send_z(j).start()

    def own_block(j):
        near_tile(j, j, False)
        if j < n_tiles - 1:
            q[...] = jnp.zeros_like(q)

            def step(i, _):
                near_tile(j, i, True)
                return 0

            lax.fori_loop(j + 1, n_tiles, step, 0)
            for n in range(TILE // 128):
                at = j * TILE + n * 128
                acc[:, at : at + 128] += mirrored(n)

    def reduce_moment():
        def arrived(k, _):
            p = peer(k)
            remote(
                rows_of(moment, p, chunk), mom_recv.at[p], mom_s.at[p], mom_r.at[p], {"sub": p}
            ).wait()
            return 0

        mom_recv[me_s] = moment[pl.ds(pl.multiple_of(me_s * chunk, chunk), chunk), :]
        lax.fori_loop(1, n_sub, arrived, 0)
        total = mom_recv[0]
        for n in range(1, n_sub):
            total = total + mom_recv[n]
        grp_src[...] = total
        grp_recv[me_g] = total

        def send(k, _):
            p = peer_g(k)
            remote(grp_src, grp_recv.at[me_g], grp_s.at[p], grp_r.at[me_g], {"grp": p}).start()
            return 0

        lax.fori_loop(1, n_grp, send, 0)

    def translate():
        def arrived(k, _):
            p = peer_g(k)
            remote(grp_src, grp_recv.at[p], grp_s.at[p], grp_r.at[p], {"grp": p}).wait()
            return 0

        lax.fori_loop(1, n_grp, arrived, 0)
        for part in range(2):
            tran_t[:, part * n_grp : part * n_grp + n_grp] = tran[part, 0].T
        coef = tran_t[pl.ds(pl.multiple_of(me_s * chunk, chunk), chunk), :]
        total = jnp.zeros((chunk, cols), F32)
        for h in range(n_grp):
            m = grp_recv[h]
            total = total + coef[:, h : h + 1] * m
            total = total + coef[:, n_grp + h : n_grp + h + 1] * lane_rotated(m)
        loc[me_s] = total.astype(BF16)

        def send(k, _):
            p = peer(k)
            remote(loc.at[me_s], loc.at[me_s], loc_s.at[p], loc_r.at[me_s], {"sub": p}).start()
            return 0

        lax.fori_loop(1, n_sub, send, 0)

    neighbour_block(0)
    reduce_moment()
    neighbour_block(1)
    translate()
    for j in range(2, n_tiles):
        neighbour_block(j)
    for j in range(n_tiles):
        own_block(j)

    def loc_arrived(k, _):
        p = peer(k)
        remote(loc.at[me_s], loc.at[p], loc_s.at[p], loc_r.at[p], {"sub": p}).wait()
        return 0

    lax.fori_loop(1, n_sub, loc_arrived, 0)
    per = 128 // chunk
    for k in range(dir_count // 128):
        block = jnp.concatenate([loc[k * per + n].astype(F32) for n in range(per)], 0)
        loc_mat[:, k * 256 : k * 256 + 128] = block.T.astype(BF16)
        loc_mat[:, k * 256 + 128 : k * 256 + 256] = (2.0 * lane_rotated(block)).T.astype(BF16)

    @pl.when(has_left)
    def _():
        for copy in halo(left):
            copy.wait_send()
        for j in range(n_tiles):
            send_z(j).wait_recv()
            acc[:, j * TILE : j * TILE + TILE] += z_recv[j].astype(F32)

    @pl.when(has_right)
    def _():
        for j in range(n_tiles):
            send_z(j).wait_send()

    near_scale = TURN * (3 * panels) ** (-0.5)
    far_scale = (dir_count * n_grp) ** (-0.5)
    partial = jnp.zeros((cols, cols), F32)
    for j in range(n_tiles):
        at = slice(j * TILE, j * TILE + TILE)
        far = jnp.dot(loc_mat[...], tables[:, at], preferred_element_type=F32)
        tile = (
            0.5 * vec[:, at].astype(F32) + near_scale * acc[:, at] + far_scale * far
        ).astype(BF16)
        applied[:, at] = tile
        partial = partial + lax.dot_general(tile, tile, NT, preferred_element_type=F32)
    partial = partial * (1.0 / (panels * n_sub * n_grp))

    n_own = cols // 8
    stride = n_sub // n_own
    mine = me_s // stride
    owner = lax.rem(me_s, stride) == 0
    gram_src[...] = partial.reshape(n_own, 8, cols)

    def gram_copy(c, slot, sem):
        return remote(
            gram_src.at[c], gram_recv.at[slot], gr_s.at[c], gr_r.at[sem], {"sub": c * stride}
        )

    def send_gram(k, _):
        c = lax.rem(mine + k, n_own)
        gram_copy(c, me_s, me_s).start()
        return 0

    lax.fori_loop(1, n_own, send_gram, 0)

    @pl.when(jnp.logical_not(owner))
    def _():
        gram_copy(mine, me_s, me_s).start()

    @pl.when(owner)
    def _():
        gram_recv[me_s] = gram_src[mine]

        def arrived(k, _):
            p = peer(k)
            gram_copy(mine, p, p).wait_recv()
            return 0

        lax.fori_loop(1, n_sub, arrived, 0)
        total = gram_recv[0]
        for n in range(1, n_sub):
            total = total + gram_recv[n]
        gsum_recv[me_g] = total

        def swap(k, _):
            p = peer_g(k)
            remote(
                gsum_recv.at[me_g], gsum_recv.at[me_g], gg_s.at[p], gg_r.at[me_g], {"grp": p}
            ).start()
            return 0

        lax.fori_loop(1, n_grp, swap, 0)

        def swapped(k, _):
            p = peer_g(k)
            remote(
                gsum_recv.at[me_g], gsum_recv.at[p], gg_s.at[p], gg_r.at[p], {"grp": p}
            ).wait()
            return 0

        lax.fori_loop(1, n_grp, swapped, 0)
        total = gsum_recv[0]
        for n in range(1, n_grp):
            total = total + gsum_recv[n]
        gram_all[mine] = total

        def spread(k, _):
            p = peer(k)
            remote(
                gram_all.at[mine], gram_all.at[mine], ga_s.at[p], ga_r.at[mine], {"sub": p}
            ).start()
            return 0

        lax.fori_loop(1, n_sub, spread, 0)

    def gathered(k, _):
        c = lax.rem(mine + k, n_own)
        remote(
            gram_all.at[c], gram_all.at[c], ga_s.at[c], ga_r.at[c], {"sub": c * stride}
        ).wait_recv()
        return 0

    lax.fori_loop(1, n_own, gathered, 0)

    @pl.when(jnp.logical_not(owner))
    def _():
        remote(
            gram_all.at[mine], gram_all.at[mine], ga_s.at[mine], ga_r.at[mine],
            {"sub": mine * stride},
        ).wait_recv()
        gram_copy(mine, me_s, me_s).wait_send()

    def sent(k, _):
        gram_copy(lax.rem(mine + k, n_own), me_s, me_s).wait_send()
        return 0

    lax.fori_loop(1, n_own, sent, 0)

    @pl.when(owner)
    def _():
        def spread_sent(k, _):
            p = peer(k)
            remote(
                gram_all.at[mine], gram_all.at[mine], ga_s.at[p], ga_r.at[mine], {"sub": p}
            ).wait_send()
            return 0

        lax.fori_loop(1, n_sub, spread_sent, 0)

    gram[...] = gram_all[...].reshape(cols, cols)


def direction_table(count):
    serial = np.arange(count).astype(np.float32)
    height = (1.0 - (2.0 * serial.astype(np.float64) + 1.0) / count)
    radius = np.sqrt(np.maximum(1.0 - height * height, 0.0))
    azimuth = (serial * np.float32(GOLDEN)).astype(np.float64)
    unit = TURN * np.stack((radius * np.cos(azimuth), radius * np.sin(azimuth), height), 1)
    table = np.zeros((count, 16), np.float64)
    for part in range(3):
        piece = unit.astype(jnp.bfloat16).astype(np.float64)
        table[:, 4 * part : 4 * part + 3] = piece
        unit = unit - piece
    return table.astype(jnp.bfloat16)


def selectors():
    table = np.zeros((16, 3 * 128), np.float32)
    for k in range(3):
        table[k, k * 128 : k * 128 + 128] = 1.0
    return table.astype(jnp.bfloat16)


def shards(n_grp, n_sub, vectors, geometry, transfer):
    cols, panels = vectors.shape
    dir_count = transfer.shape[-1]
    chunk = dir_count // n_sub
    n_tiles = panels // TILE
    n_own = cols // 8
    geo = jnp.concatenate((geometry,) * 4, 0)
    dma = pltpu.SemaphoreType.DMA
    applied, gram = pl.pallas_call(
        functools.partial(product_kernel, n_grp, n_sub),
        out_shape=(
            jax.ShapeDtypeStruct((cols, panels), BF16),
            jax.ShapeDtypeStruct((cols, cols), F32),
        ),
        in_specs=[pl.BlockSpec(memory_space=pltpu.VMEM)] * 5,
        out_specs=[pl.BlockSpec(memory_space=pltpu.VMEM)] * 2,
        scratch_shapes=[
            pltpu.VMEM((cols, panels), BF16),
            pltpu.VMEM((cols, panels), BF16),
            pltpu.VMEM((16, panels), BF16),
            pltpu.VMEM((2 * dir_count, panels), BF16),
            pltpu.VMEM((dir_count, cols), F32),
            pltpu.VMEM((n_sub, chunk, cols), F32),
            pltpu.VMEM((chunk, cols), F32),
            pltpu.VMEM((n_grp, chunk, cols), F32),
            pltpu.VMEM((dir_count, 2 * n_grp), F32),
            pltpu.VMEM((n_sub, chunk, cols), BF16),
            pltpu.VMEM((cols, 2 * dir_count), BF16),
            pltpu.VMEM((3, 8, panels), F32),
            pltpu.VMEM((3, 2 * panels, 128), F32),
            pltpu.VMEM((cols, 4 * panels), BF16),
            pltpu.VMEM((2 * TILE, TILE), BF16),
            pltpu.VMEM((cols, panels), F32),
            pltpu.VMEM((cols, 2 * TILE), F32),
            pltpu.VMEM((n_tiles, cols, TILE), BF16),
            pltpu.VMEM((n_tiles, cols, TILE), BF16),
            pltpu.VMEM((n_own, 8, cols), F32),
            pltpu.VMEM((n_sub, 8, cols), F32),
            pltpu.VMEM((n_grp, 8, cols), F32),
            pltpu.VMEM((n_own, 8, cols), F32),
            dma((2,)), dma((2,)),
            dma((n_sub,)), dma((n_sub,)),
            dma((n_grp,)), dma((n_grp,)),
            dma((n_sub,)), dma((n_sub,)),
            dma((n_tiles,)), dma((n_tiles,)),
            dma((n_own,)), dma((n_sub,)),
            dma((n_grp,)), dma((n_grp,)),
            dma((n_sub,)), dma((n_own,)),
        ],
        compiler_params=pltpu.CompilerParams(
            collective_id=0, has_side_effects=True, vmem_limit_bytes=48 << 20
        ),
    )(vectors, geo, transfer, jnp.asarray(direction_table(dir_count)), jnp.asarray(selectors()))
    lower_fac = jnp.linalg.cholesky(gram)
    ortho_basis = lax.linalg.triangular_solve(
        lower_fac, applied.astype(F32), left_side=True, lower=True
    )
    return (ortho_basis, lower_fac.T)


def solution(mesh):
    in_specs = (P(None, ("grp", "sub")), P(None, ("grp", "sub")), P(None, "grp", None, None))
    out_specs = (P(None, ("grp", "sub")), P())
    body = functools.partial(shards, mesh.shape["grp"], mesh.shape["sub"])
    return jax.shard_map(body, mesh=mesh, in_specs=in_specs, out_specs=out_specs, check_vma=False)
```

```python
import functools
import math

import jax
import jax.numpy as jnp
import numpy as np
from jax import lax
from jax.experimental import pallas as pl
from jax.experimental.pallas import tpu as pltpu
from jax.sharding import PartitionSpec as P

F32 = jnp.float32
BF16 = jnp.bfloat16
MESH = pl.DeviceIdType.MESH

KWAVE = 20.0
DELTA = 0.25
GOLDEN = math.pi * (3.0 - math.sqrt(5.0))
TURN = KWAVE / (2.0 * math.pi)
SOFT = DELTA * DELTA * TURN * TURN
Q0 = -1.03910273
P0, P1, P2 = -0.33076115, 1.40669993, -0.3346358
MAGIC = 1.5 * 2.0**23

TILE = 512
ROWS = 64
BLOCK = 16
NT = (((1,), (1,)), ((), ()))
TN = (((0,), (0,)), ((), ()))


def half_angle(t):
    f = t - ((t + MAGIC) - MAGIC)
    u = f * f
    return (P2 * u + P1) * u + P0, f * (u + Q0)


def rotated(x, axis):
    half = x.shape[axis] // 2
    re = lax.slice_in_dim(x, 0, half, axis=axis)
    im = lax.slice_in_dim(x, half, 2 * half, axis=axis)
    return jnp.concatenate((-im, re), axis)


def lane_rotated(x):
    half = x.shape[-1] // 2
    lane = lax.broadcasted_iota(jnp.int32, x.shape, x.ndim - 1)
    turned = pltpu.roll(x, half, x.ndim - 1)
    return jnp.where(lane < half, -turned, turned)


def remote(src, dst, send_sem, recv_sem, device):
    return pltpu.make_async_remote_copy(
        src_ref=src,
        dst_ref=dst,
        send_sem=send_sem,
        recv_sem=recv_sem,
        device_id=device,
        device_id_type=MESH,
    )


def product_kernel(
    n_grp, n_sub,
    vec_in, geo_in, tran_in, dirs_in,
    applied, gram,
    vec, geo_raw, tran, dirs, geo, wv, wv_nb, geo_nb, tables, moment, mom_recv, grp_src, grp_recv, tran_t, loc, loc_mat,
    xrep, yrep, w2, g, acc, q, z_send, z_recv,
    gram_src, gram_recv, gsum_recv, gram_all,
    halo_s, halo_r, mom_s, mom_r, grp_s, grp_r, loc_s, loc_r, z_s, z_r,
    gr_s, gr_r, gg_s, gg_r, ga_s, ga_r, in_s,
):
    loads = [
        pltpu.make_async_copy(src, dst, in_s.at[n])
        for n, (src, dst) in enumerate(
            ((geo_in, geo_raw), (vec_in, vec), (dirs_in, dirs), (tran_in, tran))
        )
    ]
    for load in loads:
        load.start()
    cols, panels = vec.shape
    dir_count = dirs.shape[0]
    chunk = dir_count // n_sub
    n_tiles = panels // TILE
    me_s = lax.axis_index("sub")
    me_g = lax.axis_index("grp")
    has_right = me_s < n_sub - 1
    has_left = me_s > 0

    def peer(k):
        return lax.rem(me_s + k, n_sub)

    def peer_g(k):
        return lax.rem(me_g + k, n_grp)

    barrier = pltpu.get_barrier_semaphore()

    def greet(k, _):
        pl.semaphore_signal(barrier, inc=1, device_id={"sub": peer(k)}, device_id_type=MESH)
        return 0

    lax.fori_loop(1, n_sub, greet, 0)

    def greet_g(k, _):
        pl.semaphore_signal(barrier, inc=1, device_id={"grp": peer_g(k)}, device_id_type=MESH)
        return 0

    lax.fori_loop(1, n_grp, greet_g, 0)

    for load in loads:
        load.wait()
    raw = geo_raw[...].astype(F32)
    geo[...] = jnp.concatenate((raw,) * 4, 0).astype(BF16)
    weight = geo[3:4, :].astype(F32)
    wv[...] = (vec[...].astype(F32) * weight).astype(BF16)

    pl.semaphore_wait(barrier, n_sub - 1 + n_grp - 1)

    def halo(dst_sub):
        return (
            remote(wv, wv_nb, halo_s.at[0], halo_r.at[0], {"sub": dst_sub}),
            remote(geo, geo_nb, halo_s.at[1], halo_r.at[1], {"sub": dst_sub}),
        )

    left = lax.rem(me_s + n_sub - 1, n_sub)
    right = lax.rem(me_s + 1, n_sub)

    @pl.when(has_left)
    def _():
        for copy in halo(left):
            copy.start()

    def far_tables(n, _):
        k = n // n_tiles
        col = pl.multiple_of((n % n_tiles) * TILE, TILE)
        turns = jnp.dot(
            dirs[pl.ds(pl.multiple_of(k * 128, 128), 128), :],
            geo[:, pl.ds(col, TILE)],
            preferred_element_type=F32,
        )
        a, b = half_angle(turns)
        aa, bb = a * a, b * b
        norm = aa + bb
        inv = lax.rsqrt(norm * norm)
        row = pl.multiple_of(k * 256, 256)
        tables[pl.ds(row, 128), pl.ds(col, TILE)] = ((aa - bb) * inv).astype(BF16)
        tables[pl.ds(row + 128, 128), pl.ds(col, TILE)] = (a * b * inv).astype(BF16)
        return 0

    lax.fori_loop(0, dir_count // 128 * n_tiles, far_tables, 0)

    moment_scale = (panels * n_sub) ** (-0.5)
    for k in range(dir_count // 128):
        both = lax.dot_general(
            tables[k * 256 : k * 256 + 256, :], wv[...], NT, preferred_element_type=F32
        )
        moment[k * 128 : k * 128 + 128, :] = (
            both[:128] - 2.0 * lane_rotated(both[128:])
        ) * moment_scale

    def rows_of(ref, i, size):
        return ref.at[pl.ds(pl.multiple_of(i * size, size), size), :]

    def send_moment(k, _):
        p = peer(k)
        remote(
            rows_of(moment, p, chunk), mom_recv.at[me_s], mom_s.at[p], mom_r.at[me_s], {"sub": p}
        ).start()
        return 0

    lax.fori_loop(1, n_sub, send_moment, 0)

    for k in range(3):
        xrep[k] = jnp.broadcast_to(geo[k : k + 1, :].astype(F32) * TURN, (8, panels))

    def source_side(geo_ref, wv_ref, base, offset):
        for k in range(3):
            pick = lax.broadcasted_iota(jnp.int32, (16, 128), 0) == k
            sel = jnp.where(pick, 1.0, 0.0).astype(BF16)

            def spread(n, _):
                col = pl.multiple_of(n * TILE, TILE)
                y = lax.dot_general(
                    geo_ref[:, pl.ds(col, TILE)], sel, TN,
                    preferred_element_type=F32,
                )
                if k == 0 and offset:
                    y = y + float(offset)
                yrep[k, pl.ds(base + col, TILE), :] = y * TURN
                return 0
            lax.fori_loop(0, n_tiles, spread, 0)
        for n in range(panels // 128):
            block = wv_ref[:, n * 128 : n * 128 + 128].astype(F32)
            at = 2 * base + n * 256
            w2[:, at : at + 128] = block.astype(BF16)
            w2[:, at + 128 : at + 256] = (2.0 * rotated(block, 0)).astype(BF16)

    source_side(geo, wv, 0, 0)
    acc[...] = jnp.zeros_like(acc)

    def near_tile(source, target, symmetric):
        i0 = pl.multiple_of(target * TILE, TILE)

        def strip(r, _):
            for l in range(0, TILE, 128):
                for sub in range(0, ROWS, 16):
                    row = pl.multiple_of(source * TILE + r * ROWS, ROWS) + sub

                    def diff(k):
                        y = yrep[k, pl.ds(row, 16), :].reshape(2, 8, 128)
                        return xrep[k, :, pl.ds(pl.multiple_of(i0 + l, 128), 128)] - y

                    dx, dy, dz = diff(0), diff(1), diff(2)
                    d2 = dx * dx + dy * dy + dz * dz
                    d2e = d2 + 1e-30
                    a, b = half_angle(d2e * lax.rsqrt(d2e))
                    aa, bb = a * a, b * b
                    norm = aa + bb
                    inv = lax.rsqrt(norm * norm * (d2 + SOFT))
                    at = pl.multiple_of(
                        (r * ROWS) // 128 * 256 + lax.rem(r * ROWS, 128), ROWS
                    ) + sub
                    g[pl.ds(at, 16), l : l + 128] = (
                        ((aa - bb) * inv).reshape(16, 128).astype(BF16)
                    )
                    g[pl.ds(at + 128, 16), l : l + 128] = (
                        ((a * b) * inv).reshape(16, 128).astype(BF16)
                    )
            return 0

        lax.fori_loop(0, TILE // ROWS, strip, 0)
        acc[:, pl.ds(i0, TILE)] += jnp.dot(
            w2[:, pl.ds(pl.multiple_of(source * 2 * TILE, 2 * TILE), 2 * TILE)],
            g[...],
            preferred_element_type=F32,
        )
        if symmetric:
            q[...] += lax.dot_general(
                wv[:, pl.ds(i0, TILE)], g[...], NT, preferred_element_type=F32
            )

    def mirrored(n):
        re = q[:, n * 256 : n * 256 + 128]
        im = q[:, n * 256 + 128 : n * 256 + 256]
        return re + 2.0 * rotated(im, 0)

    def send_z(j):
        return remote(z_send.at[j], z_recv.at[j], z_s.at[j], z_r.at[j], {"sub": right})

    @pl.when(has_right)
    def _():
        for copy in halo(left):
            copy.wait_recv()
        source_side(geo_nb, wv_nb, panels, 1)

    def neighbour_block(j):
        @pl.when(has_right)
        def _():
            q[...] = jnp.zeros_like(q)

            def step(i, _):
                near_tile(n_tiles + j, i, True)
                return 0

            lax.fori_loop(0, n_tiles, step, 0)
            for n in range(TILE // 128):
                z_send[j, :, n * 128 : n * 128 + 128] = mirrored(n).astype(BF16)
            send_z(j).start()

    def own_block(j):
        near_tile(j, j, False)
        if j < n_tiles - 1:
            q[...] = jnp.zeros_like(q)

            def step(i, _):
                near_tile(j, i, True)
                return 0

            lax.fori_loop(j + 1, n_tiles, step, 0)
            for n in range(TILE // 128):
                at = j * TILE + n * 128
                acc[:, at : at + 128] += mirrored(n)

    def reduce_moment():
        def arrived(k, _):
            p = peer(k)
            remote(
                rows_of(moment, p, chunk), mom_recv.at[p], mom_s.at[p], mom_r.at[p], {"sub": p}
            ).wait()
            return 0

        mom_recv[me_s] = moment[pl.ds(pl.multiple_of(me_s * chunk, chunk), chunk), :]
        lax.fori_loop(1, n_sub, arrived, 0)
        total = mom_recv[0]
        for n in range(1, n_sub):
            total = total + mom_recv[n]
        grp_src[...] = total
        grp_recv[me_g] = total

        def send(k, _):
            p = peer_g(k)
            remote(grp_src, grp_recv.at[me_g], grp_s.at[p], grp_r.at[me_g], {"grp": p}).start()
            return 0

        lax.fori_loop(1, n_grp, send, 0)

    def translate():
        def arrived(k, _):
            p = peer_g(k)
            remote(grp_src, grp_recv.at[p], grp_s.at[p], grp_r.at[p], {"grp": p}).wait()
            return 0

        lax.fori_loop(1, n_grp, arrived, 0)
        for part in range(2):
            tran_t[:, part * n_grp : part * n_grp + n_grp] = tran[part, 0].T
        coef = tran_t[pl.ds(pl.multiple_of(me_s * chunk, chunk), chunk), :]
        total = jnp.zeros((chunk, cols), F32)
        for h in range(n_grp):
            m = grp_recv[h]
            total = total + coef[:, h : h + 1] * m
            total = total + coef[:, n_grp + h : n_grp + h + 1] * lane_rotated(m)
        loc[me_s] = total.astype(BF16)

        def send(k, _):
            p = peer(k)
            remote(loc.at[me_s], loc.at[me_s], loc_s.at[p], loc_r.at[me_s], {"sub": p}).start()
            return 0

        lax.fori_loop(1, n_sub, send, 0)

    neighbour_block(0)
    reduce_moment()
    neighbour_block(1)
    translate()
    for j in range(2, n_tiles):
        neighbour_block(j)
    for j in range(n_tiles):
        own_block(j)

    def loc_arrived(k, _):
        p = peer(k)
        remote(loc.at[me_s], loc.at[p], loc_s.at[p], loc_r.at[p], {"sub": p}).wait()
        return 0

    lax.fori_loop(1, n_sub, loc_arrived, 0)
    per = 128 // chunk
    for k in range(dir_count // 128):
        block = jnp.concatenate([loc[k * per + n].astype(F32) for n in range(per)], 0)
        loc_mat[:, k * 256 : k * 256 + 128] = block.T.astype(BF16)
        loc_mat[:, k * 256 + 128 : k * 256 + 256] = (2.0 * lane_rotated(block)).T.astype(BF16)

    @pl.when(has_left)
    def _():
        for copy in halo(left):
            copy.wait_send()
        for j in range(n_tiles):
            send_z(j).wait_recv()
            acc[:, j * TILE : j * TILE + TILE] += z_recv[j].astype(F32)

    @pl.when(has_right)
    def _():
        for j in range(n_tiles):
            send_z(j).wait_send()

    near_scale = TURN * (3 * panels) ** (-0.5)
    far_scale = (dir_count * n_grp) ** (-0.5)
    partial = jnp.zeros((cols, cols), F32)
    for j in range(n_tiles):
        at = slice(j * TILE, j * TILE + TILE)
        far = jnp.dot(loc_mat[...], tables[:, at], preferred_element_type=F32)
        tile = (
            0.5 * vec[:, at].astype(F32) + near_scale * acc[:, at] + far_scale * far
        ).astype(BF16)
        applied[:, at] = tile
        partial = partial + lax.dot_general(tile, tile, NT, preferred_element_type=F32)
    partial = partial * (1.0 / (panels * n_sub * n_grp))

    n_own = cols // 8
    stride = n_sub // n_own
    mine = me_s // stride
    owner = lax.rem(me_s, stride) == 0
    gram_src[...] = partial.reshape(n_own, 8, cols)

    def gram_copy(c, slot, sem):
        return remote(
            gram_src.at[c], gram_recv.at[slot], gr_s.at[c], gr_r.at[sem], {"sub": c * stride}
        )

    def send_gram(k, _):
        c = lax.rem(mine + k, n_own)
        gram_copy(c, me_s, me_s).start()
        return 0

    lax.fori_loop(1, n_own, send_gram, 0)

    @pl.when(jnp.logical_not(owner))
    def _():
        gram_copy(mine, me_s, me_s).start()

    @pl.when(owner)
    def _():
        gram_recv[me_s] = gram_src[mine]

        def arrived(k, _):
            p = peer(k)
            gram_copy(mine, p, p).wait_recv()
            return 0

        lax.fori_loop(1, n_sub, arrived, 0)
        total = gram_recv[0]
        for n in range(1, n_sub):
            total = total + gram_recv[n]
        gsum_recv[me_g] = total

        def swap(k, _):
            p = peer_g(k)
            remote(
                gsum_recv.at[me_g], gsum_recv.at[me_g], gg_s.at[p], gg_r.at[me_g], {"grp": p}
            ).start()
            return 0

        lax.fori_loop(1, n_grp, swap, 0)

        def swapped(k, _):
            p = peer_g(k)
            remote(
                gsum_recv.at[me_g], gsum_recv.at[p], gg_s.at[p], gg_r.at[p], {"grp": p}
            ).wait()
            return 0

        lax.fori_loop(1, n_grp, swapped, 0)
        total = gsum_recv[0]
        for n in range(1, n_grp):
            total = total + gsum_recv[n]
        gram_all[mine] = total

        def spread(k, _):
            p = peer(k)
            remote(
                gram_all.at[mine], gram_all.at[mine], ga_s.at[p], ga_r.at[mine], {"sub": p}
            ).start()
            return 0

        lax.fori_loop(1, n_sub, spread, 0)

    def gathered(k, _):
        c = lax.rem(mine + k, n_own)
        remote(
            gram_all.at[c], gram_all.at[c], ga_s.at[c], ga_r.at[c], {"sub": c * stride}
        ).wait_recv()
        return 0

    lax.fori_loop(1, n_own, gathered, 0)

    @pl.when(jnp.logical_not(owner))
    def _():
        remote(
            gram_all.at[mine], gram_all.at[mine], ga_s.at[mine], ga_r.at[mine],
            {"sub": mine * stride},
        ).wait_recv()
        gram_copy(mine, me_s, me_s).wait_send()

    def sent(k, _):
        gram_copy(lax.rem(mine + k, n_own), me_s, me_s).wait_send()
        return 0

    lax.fori_loop(1, n_own, sent, 0)

    @pl.when(owner)
    def _():
        def spread_sent(k, _):
            p = peer(k)
            remote(
                gram_all.at[mine], gram_all.at[mine], ga_s.at[p], ga_r.at[mine], {"sub": p}
            ).wait_send()
            return 0

        lax.fori_loop(1, n_sub, spread_sent, 0)

    gram[...] = gram_all[...].reshape(cols, cols)


def factor_kernel(gram, applied, ortho, upper, work, inverse):
    n = gram.shape[0]
    work[...] = gram[...]
    sub = lax.broadcasted_iota(jnp.int32, (BLOCK, n), 0)
    lane = lax.broadcasted_iota(jnp.int32, (BLOCK, n), 1)
    for k in range(0, n, BLOCK):
        rows = work[k : k + BLOCK, :]
        col = [jnp.broadcast_to(rows[:, k + j : k + j + 1], (BLOCK, n)) for j in range(BLOCK)]
        inside = (lane >= k) & (lane < k + BLOCK)
        panel = jnp.where(inside, jnp.where(lane - k == sub, 1.0, 0.0), rows)
        scale = jnp.ones((BLOCK, n), F32)
        for j in range(BLOCK):
            root = lax.rsqrt(jnp.broadcast_to(col[j][j : j + 1, :], (BLOCK, n)))
            scale = jnp.where(sub == j, root, scale)
            if j < BLOCK - 1:
                ratio = jnp.where(sub > j, col[j] * (root * root), 0.0)
                for l in range(j + 1, BLOCK):
                    col[l] = col[l] - ratio * jnp.broadcast_to(col[l][j : j + 1, :], (BLOCK, n))
                panel = panel - ratio * jnp.broadcast_to(panel[j : j + 1, :], (BLOCK, n))
        panel = panel * scale
        inverse[k : k + BLOCK, :] = jnp.where(lane < k + BLOCK, panel, 0.0)
        corner = jnp.zeros((BLOCK, n), F32)
        for j in range(BLOCK):
            corner = jnp.where((lane == k + j) & (sub <= j), col[j], corner)
        upper[k : k + BLOCK, :] = jnp.where(lane >= k + BLOCK, panel, corner * scale)
        if k + BLOCK < n:
            hi = panel.astype(BF16).astype(F32)
            rest = panel - hi
            mid = rest.astype(BF16).astype(F32)
            lo = rest - mid
            left = jnp.concatenate((hi, hi, mid, hi, lo, mid), 0).astype(BF16)
            right = jnp.concatenate((hi, mid, hi, lo, hi, mid), 0).astype(BF16)
            update = lax.dot_general(left, right, TN, preferred_element_type=F32)
            below = work[k + BLOCK :, :]
            at = lax.broadcasted_iota(jnp.int32, below.shape, 1)
            below = jnp.where((at >= k) & (at < k + BLOCK), 0.0, below)
            work[k + BLOCK :, :] = below - update[k + BLOCK :, :]
    whole = inverse[...]
    hi = whole.astype(BF16)
    lo = (whole - hi.astype(F32)).astype(BF16)
    for c in range(0, applied.shape[1], TILE):
        tile = applied[:, c : c + TILE]
        ortho[:, c : c + TILE] = jnp.dot(hi, tile, preferred_element_type=F32) + jnp.dot(
            lo, tile, preferred_element_type=F32
        )


def direction_table(count):
    serial = np.arange(count).astype(np.float32)
    height = (1.0 - (2.0 * serial.astype(np.float64) + 1.0) / count)
    radius = np.sqrt(np.maximum(1.0 - height * height, 0.0))
    azimuth = (serial * np.float32(GOLDEN)).astype(np.float64)
    unit = TURN * np.stack((radius * np.cos(azimuth), radius * np.sin(azimuth), height), 1)
    table = np.zeros((count, 16), np.float64)
    for part in range(3):
        piece = unit.astype(jnp.bfloat16).astype(np.float64)
        table[:, 4 * part : 4 * part + 3] = piece
        unit = unit - piece
    return table.astype(jnp.bfloat16)


def shards(n_grp, n_sub, vectors, geometry, transfer):
    cols, panels = vectors.shape
    dir_count = transfer.shape[-1]
    chunk = dir_count // n_sub
    n_tiles = panels // TILE
    n_own = cols // 8
    dma = pltpu.SemaphoreType.DMA
    applied, gram = pl.pallas_call(
        functools.partial(product_kernel, n_grp, n_sub),
        out_shape=(
            jax.ShapeDtypeStruct((cols, panels), BF16),
            jax.ShapeDtypeStruct((cols, cols), F32),
        ),
        in_specs=[pl.BlockSpec(memory_space=pl.ANY)] * 4,
        out_specs=[pl.BlockSpec(memory_space=pltpu.VMEM)] * 2,
        scratch_shapes=[
            pltpu.VMEM((cols, panels), BF16),
            pltpu.VMEM((4, panels), BF16),
            pltpu.VMEM(transfer.shape, F32),
            pltpu.VMEM((dir_count, 16), BF16),
            pltpu.VMEM((16, panels), BF16),
            pltpu.VMEM((cols, panels), BF16),
            pltpu.VMEM((cols, panels), BF16),
            pltpu.VMEM((16, panels), BF16),
            pltpu.VMEM((2 * dir_count, panels), BF16),
            pltpu.VMEM((dir_count, cols), F32),
            pltpu.VMEM((n_sub, chunk, cols), F32),
            pltpu.VMEM((chunk, cols), F32),
            pltpu.VMEM((n_grp, chunk, cols), F32),
            pltpu.VMEM((dir_count, 2 * n_grp), F32),
            pltpu.VMEM((n_sub, chunk, cols), BF16),
            pltpu.VMEM((cols, 2 * dir_count), BF16),
            pltpu.VMEM((3, 8, panels), F32),
            pltpu.VMEM((3, 2 * panels, 128), F32),
            pltpu.VMEM((cols, 4 * panels), BF16),
            pltpu.VMEM((2 * TILE, TILE), BF16),
            pltpu.VMEM((cols, panels), F32),
            pltpu.VMEM((cols, 2 * TILE), F32),
            pltpu.VMEM((n_tiles, cols, TILE), BF16),
            pltpu.VMEM((n_tiles, cols, TILE), BF16),
            pltpu.VMEM((n_own, 8, cols), F32),
            pltpu.VMEM((n_sub, 8, cols), F32),
            pltpu.VMEM((n_grp, 8, cols), F32),
            pltpu.VMEM((n_own, 8, cols), F32),
            dma((2,)), dma((2,)),
            dma((n_sub,)), dma((n_sub,)),
            dma((n_grp,)), dma((n_grp,)),
            dma((n_sub,)), dma((n_sub,)),
            dma((n_tiles,)), dma((n_tiles,)),
            dma((n_own,)), dma((n_sub,)),
            dma((n_grp,)), dma((n_grp,)),
            dma((n_sub,)), dma((n_own,)),
            dma((4,)),
        ],
        compiler_params=pltpu.CompilerParams(
            collective_id=0, has_side_effects=True, vmem_limit_bytes=56 << 20
        ),
    )(vectors, geometry, transfer, jnp.asarray(direction_table(dir_count)))
    return tuple(
        pl.pallas_call(
            factor_kernel,
            out_shape=(
                jax.ShapeDtypeStruct((cols, panels), F32),
                jax.ShapeDtypeStruct((cols, cols), F32),
            ),
            in_specs=[pl.BlockSpec(memory_space=pltpu.VMEM)] * 2,
            out_specs=[pl.BlockSpec(memory_space=pltpu.VMEM)] * 2,
            scratch_shapes=[pltpu.VMEM((cols, cols), F32)] * 2,
            compiler_params=pltpu.CompilerParams(vmem_limit_bytes=16 << 20),
        )(gram, applied)
    )


def solution(mesh):
    in_specs = (P(None, ("grp", "sub")), P(None, ("grp", "sub")), P(None, "grp", None, None))
    out_specs = (P(None, ("grp", "sub")), P())
    body = functools.partial(shards, mesh.shape["grp"], mesh.shape["sub"])
    return jax.shard_map(body, mesh=mesh, in_specs=in_specs, out_specs=out_specs, check_vma=False)
```

```python
import functools
import math

import jax
import jax.numpy as jnp
import numpy as np
from jax import lax
from jax.experimental import pallas as pl
from jax.experimental.pallas import tpu as pltpu
from jax.sharding import PartitionSpec as P

F32 = jnp.float32
BF16 = jnp.bfloat16
MESH = pl.DeviceIdType.MESH

KWAVE = 20.0
DELTA = 0.25
GOLDEN = math.pi * (3.0 - math.sqrt(5.0))
TURN = KWAVE / (2.0 * math.pi)
SOFT = DELTA * DELTA * TURN * TURN
Q0 = -1.03910273
P0, P1, P2 = -0.33076115, 1.40669993, -0.3346358
MAGIC = 1.5 * 2.0**23

TILE = 512
ROWS = 64
BLOCK = 16
NT = (((1,), (1,)), ((), ()))
TN = (((0,), (0,)), ((), ()))


def half_angle(t):
    f = t - ((t + MAGIC) - MAGIC)
    u = f * f
    return (P2 * u + P1) * u + P0, f * (u + Q0)


def rotated(x, axis):
    half = x.shape[axis] // 2
    re = lax.slice_in_dim(x, 0, half, axis=axis)
    im = lax.slice_in_dim(x, half, 2 * half, axis=axis)
    return jnp.concatenate((-im, re), axis)


def lane_rotated(x):
    half = x.shape[-1] // 2
    lane = lax.broadcasted_iota(jnp.int32, x.shape, x.ndim - 1)
    turned = pltpu.roll(x, half, x.ndim - 1)
    return jnp.where(lane < half, -turned, turned)


def remote(src, dst, send_sem, recv_sem, device):
    return pltpu.make_async_remote_copy(
        src_ref=src,
        dst_ref=dst,
        send_sem=send_sem,
        recv_sem=recv_sem,
        device_id=device,
        device_id_type=MESH,
    )


def product_kernel(
    n_grp, n_sub,
    vec_in, geo_in, tran_in, dirs_in,
    applied, gram,
    vec, geo_raw, tran, dirs, geo, wv, wv_nb, geo_nb, tables, moment, mom_recv, grp_src, grp_recv, tran_t, loc, loc_mat,
    xrep, yrep, g, acc, z_acc, z_send, z_recv,
    gram_src, gram_recv, gsum_recv, gram_all,
    halo_s, halo_r, mom_s, mom_r, grp_s, grp_r, loc_s, loc_r, z_s, z_r,
    gr_s, gr_r, gg_s, gg_r, ga_s, ga_r, in_s,
):
    loads = [
        pltpu.make_async_copy(src, dst, in_s.at[n])
        for n, (src, dst) in enumerate(
            ((geo_in, geo_raw), (vec_in, vec), (dirs_in, dirs), (tran_in, tran))
        )
    ]
    for load in loads:
        load.start()
    cols, panels = vec.shape
    dir_count = dirs.shape[0]
    chunk = dir_count // n_sub
    n_tiles = panels // TILE
    me_s = lax.axis_index("sub")
    me_g = lax.axis_index("grp")
    has_right = me_s < n_sub - 1
    has_left = me_s > 0

    def peer(k):
        return lax.rem(me_s + k, n_sub)

    def peer_g(k):
        return lax.rem(me_g + k, n_grp)

    barrier = pltpu.get_barrier_semaphore()

    def greet(k, _):
        pl.semaphore_signal(barrier, inc=1, device_id={"sub": peer(k)}, device_id_type=MESH)
        return 0

    lax.fori_loop(1, n_sub, greet, 0)

    def greet_g(k, _):
        pl.semaphore_signal(barrier, inc=1, device_id={"grp": peer_g(k)}, device_id_type=MESH)
        return 0

    lax.fori_loop(1, n_grp, greet_g, 0)

    for load in loads:
        load.wait()
    raw = geo_raw[...].astype(F32)
    geo[...] = jnp.concatenate((raw,) * 4, 0).astype(BF16)
    weight = geo[3:4, :].astype(F32)
    wv[...] = (vec[...].astype(F32) * weight).astype(BF16)

    def halo(dst_sub):
        return (
            remote(wv, wv_nb, halo_s.at[0], halo_r.at[0], {"sub": dst_sub}),
            remote(geo, geo_nb, halo_s.at[1], halo_r.at[1], {"sub": dst_sub}),
        )

    left = lax.rem(me_s + n_sub - 1, n_sub)
    right = lax.rem(me_s + 1, n_sub)

    half = panels // 2

    def far_tables(n, _):
        k = n // 2
        col = pl.multiple_of((n % 2) * half, half)
        turns = jnp.dot(
            dirs[pl.ds(pl.multiple_of(k * 128, 128), 128), :],
            geo[:, pl.ds(col, half)],
            preferred_element_type=F32,
        )
        a, b = half_angle(turns)
        aa, bb = a * a, b * b
        norm = aa + bb
        inv = lax.rsqrt(norm * norm)
        row = pl.multiple_of(k * 256, 256)
        tables[pl.ds(row, 128), pl.ds(col, half)] = ((aa - bb) * inv).astype(BF16)
        tables[pl.ds(row + 128, 128), pl.ds(col, half)] = (a * b * inv).astype(BF16)
        return 0

    lax.fori_loop(0, dir_count // 128 * 2, far_tables, 0)

    pl.semaphore_wait(barrier, n_sub - 1 + n_grp - 1)

    @pl.when(has_left)
    def _():
        for copy in halo(left):
            copy.start()

    moment_scale = (panels * n_sub) ** (-0.5)
    for k in range(dir_count // 128):
        both = lax.dot_general(
            tables[k * 256 : k * 256 + 256, :], wv[...], NT, preferred_element_type=F32
        )
        moment[k * 128 : k * 128 + 128, :] = (
            both[:128] - 2.0 * lane_rotated(both[128:])
        ) * moment_scale

    def rows_of(ref, i, size):
        return ref.at[pl.ds(pl.multiple_of(i * size, size), size), :]

    def send_moment(k, _):
        p = peer(k)
        remote(
            rows_of(moment, p, chunk), mom_recv.at[me_s], mom_s.at[p], mom_r.at[me_s], {"sub": p}
        ).start()
        return 0

    lax.fori_loop(1, n_sub, send_moment, 0)

    for k in range(3):
        xrep[k] = jnp.broadcast_to(geo[k : k + 1, :].astype(F32) * TURN, (8, panels))

    def source_side(geo_ref, base, offset):
        rows = lax.broadcasted_iota(jnp.int32, (16, 3 * 128), 0)
        lanes = lax.broadcasted_iota(jnp.int32, (16, 3 * 128), 1)
        pick = (lanes >= rows * 128) & (lanes < rows * 128 + 128)
        sel = jnp.where(pick, 1.0, 0.0).astype(BF16)

        for col in range(0, panels, TILE):
            y = lax.dot_general(
                geo_ref[:, col : col + TILE], sel, TN, preferred_element_type=F32
            )
            for k in range(3):
                part = y[:, k * 128 : k * 128 + 128]
                if k == 0 and offset:
                    part = part + float(offset)
                yrep[k, base + col : base + col + TILE, :] = part * TURN

    source_side(geo, 0, 0)
    acc[...] = jnp.zeros_like(acc)

    def near_tile(source, target, weighted, mirror):
        i0 = pl.multiple_of(target * TILE, TILE)

        def strip(r, _):
            for l in range(0, TILE, 128):
                for sub in range(0, ROWS, 16):
                    row = pl.multiple_of(source * TILE + r * ROWS, ROWS) + sub

                    def diff(k):
                        y = yrep[k, pl.ds(row, 16), :].reshape(2, 8, 128)
                        return xrep[k, :, pl.ds(pl.multiple_of(i0 + l, 128), 128)] - y

                    dx, dy, dz = diff(0), diff(1), diff(2)
                    d2 = dx * dx + dy * dy + dz * dz
                    d2e = d2 + 1e-30
                    a, b = half_angle(d2e * lax.rsqrt(d2e))
                    aa, bb = a * a, b * b
                    norm = aa + bb
                    inv = lax.rsqrt(norm * norm * (d2 + SOFT))
                    at = pl.multiple_of(r * ROWS, ROWS) + sub
                    g[pl.ds(at, 16), l : l + 128] = (
                        ((aa - bb) * inv).reshape(16, 128).astype(BF16)
                    )
                    g[pl.ds(at + TILE, 16), l : l + 128] = (
                        ((a * b) * inv).reshape(16, 128).astype(BF16)
                    )
            return 0

        lax.fori_loop(0, TILE // ROWS, strip, 0)
        for part in range(2):
            acc[part * cols : part * cols + cols, pl.ds(i0, TILE)] += jnp.dot(
                weighted, g[part * TILE : part * TILE + TILE, :], preferred_element_type=F32
            )
        if mirror is not None:
            ref, at = mirror
            for part in range(2):
                ref[part * cols : part * cols + cols, at : at + TILE] += lax.dot_general(
                    wv[:, pl.ds(i0, TILE)], g[part * TILE : part * TILE + TILE, :], NT,
                    preferred_element_type=F32,
                )

    def joined(re, im):
        return re + 2.0 * rotated(im, 0)

    def send_z(j):
        return remote(z_send.at[j], z_recv.at[j], z_s.at[j], z_r.at[j], {"sub": right})

    def neighbour_start():
        @pl.when(has_right)
        def _():
            for copy in halo(left):
                copy.wait_recv()
            source_side(geo_nb, panels, 1)

    def neighbour_block(j):
        @pl.when(has_right)
        def _():
            z_acc[...] = jnp.zeros_like(z_acc)

            def step(i, _):
                near_tile(n_tiles + j, i, wv_nb[:, j * TILE : j * TILE + TILE], (z_acc, 0))
                return 0

            lax.fori_loop(0, n_tiles, step, 0)
            z_send[j] = joined(z_acc[:cols], z_acc[cols:]).astype(BF16)
            send_z(j).start()

    def own_block(j):
        weighted = wv[:, j * TILE : j * TILE + TILE]
        near_tile(j, j, weighted, None)
        if j < n_tiles - 1:

            def step(i, _):
                near_tile(j, i, weighted, (acc, j * TILE))
                return 0

            lax.fori_loop(j + 1, n_tiles, step, 0)

    def reduce_moment():
        def arrived(k, _):
            p = peer(k)
            remote(
                rows_of(moment, p, chunk), mom_recv.at[p], mom_s.at[p], mom_r.at[p], {"sub": p}
            ).wait()
            return 0

        mom_recv[me_s] = moment[pl.ds(pl.multiple_of(me_s * chunk, chunk), chunk), :]
        lax.fori_loop(1, n_sub, arrived, 0)
        total = mom_recv[0]
        for n in range(1, n_sub):
            total = total + mom_recv[n]
        grp_src[...] = total
        grp_recv[me_g] = total

        def send(k, _):
            p = peer_g(k)
            remote(grp_src, grp_recv.at[me_g], grp_s.at[p], grp_r.at[me_g], {"grp": p}).start()
            return 0

        lax.fori_loop(1, n_grp, send, 0)

    def translate():
        def arrived(k, _):
            p = peer_g(k)
            remote(grp_src, grp_recv.at[p], grp_s.at[p], grp_r.at[p], {"grp": p}).wait()
            return 0

        lax.fori_loop(1, n_grp, arrived, 0)
        for part in range(2):
            tran_t[:, part * n_grp : part * n_grp + n_grp] = tran[part, 0].T
        coef = tran_t[pl.ds(pl.multiple_of(me_s * chunk, chunk), chunk), :]
        total = jnp.zeros((chunk, cols), F32)
        for h in range(n_grp):
            m = grp_recv[h]
            total = total + coef[:, h : h + 1] * m
            total = total + coef[:, n_grp + h : n_grp + h + 1] * lane_rotated(m)
        loc[me_s] = total.astype(BF16)

        def send(k, _):
            p = peer(k)
            remote(loc.at[me_s], loc.at[me_s], loc_s.at[p], loc_r.at[me_s], {"sub": p}).start()
            return 0

        lax.fori_loop(1, n_sub, send, 0)

    own_block(0)
    neighbour_start()
    neighbour_block(0)
    reduce_moment()
    neighbour_block(1)
    translate()
    for j in range(2, n_tiles):
        neighbour_block(j)
    for j in range(1, n_tiles):
        own_block(j)

    def loc_arrived(k, _):
        p = peer(k)
        remote(loc.at[me_s], loc.at[p], loc_s.at[p], loc_r.at[p], {"sub": p}).wait()
        return 0

    lax.fori_loop(1, n_sub, loc_arrived, 0)
    per = 128 // chunk
    for k in range(dir_count // 128):
        block = jnp.concatenate([loc[k * per + n].astype(F32) for n in range(per)], 0)
        loc_mat[:, k * 256 : k * 256 + 128] = block.T.astype(BF16)
        loc_mat[:, k * 256 + 128 : k * 256 + 256] = (2.0 * lane_rotated(block)).T.astype(BF16)

    @pl.when(has_left)
    def _():
        for copy in halo(left):
            copy.wait_send()
        for j in range(n_tiles):
            send_z(j).wait_recv()
            acc[:cols, j * TILE : j * TILE + TILE] += z_recv[j].astype(F32)

    @pl.when(has_right)
    def _():
        for j in range(n_tiles):
            send_z(j).wait_send()

    near_scale = TURN * (3 * panels) ** (-0.5)
    far_scale = (dir_count * n_grp) ** (-0.5)
    partial = jnp.zeros((cols, cols), F32)
    for j in range(n_tiles):
        at = slice(j * TILE, j * TILE + TILE)
        far = jnp.dot(loc_mat[...], tables[:, at], preferred_element_type=F32)
        tile = (
            0.5 * vec[:, at].astype(F32) + near_scale * joined(acc[:cols, at], acc[cols:, at]) + far_scale * far
        ).astype(BF16)
        applied[:, at] = tile
        partial = partial + lax.dot_general(tile, tile, NT, preferred_element_type=F32)
    partial = partial * (1.0 / (panels * n_sub * n_grp))

    n_own = cols // 8
    stride = n_sub // n_own
    mine = me_s // stride
    owner = lax.rem(me_s, stride) == 0
    gram_src[...] = partial.reshape(n_own, 8, cols)

    def gram_copy(c, slot, sem):
        return remote(
            gram_src.at[c], gram_recv.at[slot], gr_s.at[c], gr_r.at[sem], {"sub": c * stride}
        )

    def send_gram(k, _):
        c = lax.rem(mine + k, n_own)
        gram_copy(c, me_s, me_s).start()
        return 0

    lax.fori_loop(1, n_own, send_gram, 0)

    @pl.when(jnp.logical_not(owner))
    def _():
        gram_copy(mine, me_s, me_s).start()

    @pl.when(owner)
    def _():
        gram_recv[me_s] = gram_src[mine]

        def arrived(k, _):
            p = peer(k)
            gram_copy(mine, p, p).wait_recv()
            return 0

        lax.fori_loop(1, n_sub, arrived, 0)
        total = gram_recv[0]
        for n in range(1, n_sub):
            total = total + gram_recv[n]
        gsum_recv[me_g] = total

        def swap(k, _):
            p = peer_g(k)
            remote(
                gsum_recv.at[me_g], gsum_recv.at[me_g], gg_s.at[p], gg_r.at[me_g], {"grp": p}
            ).start()
            return 0

        lax.fori_loop(1, n_grp, swap, 0)

        def swapped(k, _):
            p = peer_g(k)
            remote(
                gsum_recv.at[me_g], gsum_recv.at[p], gg_s.at[p], gg_r.at[p], {"grp": p}
            ).wait()
            return 0

        lax.fori_loop(1, n_grp, swapped, 0)
        total = gsum_recv[0]
        for n in range(1, n_grp):
            total = total + gsum_recv[n]
        gram_all[mine] = total

        def spread(k, _):
            p = peer(k)
            remote(
                gram_all.at[mine], gram_all.at[mine], ga_s.at[p], ga_r.at[mine], {"sub": p}
            ).start()
            return 0

        lax.fori_loop(1, n_sub, spread, 0)

    def gathered(k, _):
        c = lax.rem(mine + k, n_own)
        remote(
            gram_all.at[c], gram_all.at[c], ga_s.at[c], ga_r.at[c], {"sub": c * stride}
        ).wait_recv()
        return 0

    lax.fori_loop(1, n_own, gathered, 0)

    @pl.when(jnp.logical_not(owner))
    def _():
        remote(
            gram_all.at[mine], gram_all.at[mine], ga_s.at[mine], ga_r.at[mine],
            {"sub": mine * stride},
        ).wait_recv()
        gram_copy(mine, me_s, me_s).wait_send()

    def sent(k, _):
        gram_copy(lax.rem(mine + k, n_own), me_s, me_s).wait_send()
        return 0

    lax.fori_loop(1, n_own, sent, 0)

    @pl.when(owner)
    def _():
        def spread_sent(k, _):
            p = peer(k)
            remote(
                gram_all.at[mine], gram_all.at[mine], ga_s.at[p], ga_r.at[mine], {"sub": p}
            ).wait_send()
            return 0

        lax.fori_loop(1, n_sub, spread_sent, 0)

    gram[...] = gram_all[...].reshape(cols, cols)


def factor_kernel(gram, applied_in, ortho, upper, work, inverse, applied, sems):
    n = gram.shape[0]
    load_gram = pltpu.make_async_copy(gram, work, sems.at[0])
    load_applied = pltpu.make_async_copy(applied_in, applied, sems.at[1])
    load_gram.start()
    load_applied.start()
    load_gram.wait()
    sub = lax.broadcasted_iota(jnp.int32, (BLOCK, n), 0)
    lane = lax.broadcasted_iota(jnp.int32, (BLOCK, n), 1)
    for k in range(0, n, BLOCK):
        rows = work[k : k + BLOCK, :]
        col = [jnp.broadcast_to(rows[:, k + j : k + j + 1], (BLOCK, n)) for j in range(BLOCK)]
        inside = (lane >= k) & (lane < k + BLOCK)
        panel = jnp.where(inside, jnp.where(lane - k == sub, 1.0, 0.0), rows)
        scale = jnp.ones((BLOCK, n), F32)
        for j in range(BLOCK):
            root = lax.rsqrt(jnp.broadcast_to(col[j][j : j + 1, :], (BLOCK, n)))
            scale = jnp.where(sub == j, root, scale)
            if j < BLOCK - 1:
                ratio = jnp.where(sub > j, col[j] * (root * root), 0.0)
                for l in range(j + 1, BLOCK):
                    col[l] = col[l] - ratio * jnp.broadcast_to(col[l][j : j + 1, :], (BLOCK, n))
                panel = panel - ratio * jnp.broadcast_to(panel[j : j + 1, :], (BLOCK, n))
        panel = panel * scale
        inverse[k : k + BLOCK, :] = jnp.where(lane < k + BLOCK, panel, 0.0)
        corner = jnp.zeros((BLOCK, n), F32)
        for j in range(BLOCK):
            corner = jnp.where((lane == k + j) & (sub <= j), col[j], corner)
        upper[k : k + BLOCK, :] = jnp.where(lane >= k + BLOCK, panel, corner * scale)
        if k + BLOCK < n:
            hi = panel.astype(BF16).astype(F32)
            rest = panel - hi
            mid = rest.astype(BF16).astype(F32)
            lo = rest - mid
            left = jnp.concatenate((hi, hi, mid, hi, lo, mid), 0).astype(BF16)
            right = jnp.concatenate((hi, mid, hi, lo, hi, mid), 0).astype(BF16)
            update = lax.dot_general(left, right, TN, preferred_element_type=F32)
            below = work[k + BLOCK :, :]
            at = lax.broadcasted_iota(jnp.int32, below.shape, 1)
            below = jnp.where((at >= k) & (at < k + BLOCK), 0.0, below)
            work[k + BLOCK :, :] = below - update[k + BLOCK :, :]
    load_applied.wait()
    whole = inverse[...]
    hi = whole.astype(BF16)
    lo = (whole - hi.astype(F32)).astype(BF16)
    for c in range(0, applied.shape[1], TILE):
        tile = applied[:, c : c + TILE]
        ortho[:, c : c + TILE] = jnp.dot(hi, tile, preferred_element_type=F32) + jnp.dot(
            lo, tile, preferred_element_type=F32
        )


def direction_table(count):
    serial = np.arange(count).astype(np.float32)
    height = (1.0 - (2.0 * serial.astype(np.float64) + 1.0) / count)
    radius = np.sqrt(np.maximum(1.0 - height * height, 0.0))
    azimuth = (serial * np.float32(GOLDEN)).astype(np.float64)
    unit = TURN * np.stack((radius * np.cos(azimuth), radius * np.sin(azimuth), height), 1)
    table = np.zeros((count, 16), np.float64)
    for part in range(3):
        piece = unit.astype(jnp.bfloat16).astype(np.float64)
        table[:, 4 * part : 4 * part + 3] = piece
        unit = unit - piece
    return table.astype(jnp.bfloat16)


def shards(n_grp, n_sub, vectors, geometry, transfer):
    cols, panels = vectors.shape
    dir_count = transfer.shape[-1]
    chunk = dir_count // n_sub
    n_tiles = panels // TILE
    n_own = cols // 8
    dma = pltpu.SemaphoreType.DMA
    applied, gram = pl.pallas_call(
        functools.partial(product_kernel, n_grp, n_sub),
        out_shape=(
            jax.ShapeDtypeStruct((cols, panels), BF16),
            jax.ShapeDtypeStruct((cols, cols), F32),
        ),
        in_specs=[pl.BlockSpec(memory_space=pl.ANY)] * 4,
        out_specs=[pl.BlockSpec(memory_space=pltpu.VMEM)] * 2,
        scratch_shapes=[
            pltpu.VMEM((cols, panels), BF16),
            pltpu.VMEM((4, panels), BF16),
            pltpu.VMEM(transfer.shape, F32),
            pltpu.VMEM((dir_count, 16), BF16),
            pltpu.VMEM((16, panels), BF16),
            pltpu.VMEM((cols, panels), BF16),
            pltpu.VMEM((cols, panels), BF16),
            pltpu.VMEM((16, panels), BF16),
            pltpu.VMEM((2 * dir_count, panels), BF16),
            pltpu.VMEM((dir_count, cols), F32),
            pltpu.VMEM((n_sub, chunk, cols), F32),
            pltpu.VMEM((chunk, cols), F32),
            pltpu.VMEM((n_grp, chunk, cols), F32),
            pltpu.VMEM((dir_count, 2 * n_grp), F32),
            pltpu.VMEM((n_sub, chunk, cols), BF16),
            pltpu.VMEM((cols, 2 * dir_count), BF16),
            pltpu.VMEM((3, 8, panels), F32),
            pltpu.VMEM((3, 2 * panels, 128), F32),
            pltpu.VMEM((2 * TILE, TILE), BF16),
            pltpu.VMEM((2 * cols, panels), F32),
            pltpu.VMEM((2 * cols, TILE), F32),
            pltpu.VMEM((n_tiles, cols, TILE), BF16),
            pltpu.VMEM((n_tiles, cols, TILE), BF16),
            pltpu.VMEM((n_own, 8, cols), F32),
            pltpu.VMEM((n_sub, 8, cols), F32),
            pltpu.VMEM((n_grp, 8, cols), F32),
            pltpu.VMEM((n_own, 8, cols), F32),
            dma((2,)), dma((2,)),
            dma((n_sub,)), dma((n_sub,)),
            dma((n_grp,)), dma((n_grp,)),
            dma((n_sub,)), dma((n_sub,)),
            dma((n_tiles,)), dma((n_tiles,)),
            dma((n_own,)), dma((n_sub,)),
            dma((n_grp,)), dma((n_grp,)),
            dma((n_sub,)), dma((n_own,)),
            dma((4,)),
        ],
        compiler_params=pltpu.CompilerParams(
            collective_id=0, has_side_effects=True, vmem_limit_bytes=56 << 20
        ),
    )(vectors, geometry, transfer, jnp.asarray(direction_table(dir_count)))
    return tuple(
        pl.pallas_call(
            factor_kernel,
            out_shape=(
                jax.ShapeDtypeStruct((cols, panels), F32),
                jax.ShapeDtypeStruct((cols, cols), F32),
            ),
            in_specs=[pl.BlockSpec(memory_space=pl.ANY)] * 2,
            out_specs=[pl.BlockSpec(memory_space=pltpu.VMEM)] * 2,
            scratch_shapes=[
                pltpu.VMEM((cols, cols), F32),
                pltpu.VMEM((cols, cols), F32),
                pltpu.VMEM((cols, panels), BF16),
                dma((2,)),
            ],
            compiler_params=pltpu.CompilerParams(vmem_limit_bytes=56 << 20),
        )(gram, applied)
    )


def solution(mesh):
    in_specs = (P(None, ("grp", "sub")), P(None, ("grp", "sub")), P(None, "grp", None, None))
    out_specs = (P(None, ("grp", "sub")), P())
    body = functools.partial(shards, mesh.shape["grp"], mesh.shape["sub"])
    return jax.shard_map(body, mesh=mesh, in_specs=in_specs, out_specs=out_specs, check_vma=False)
```

```python
import functools
import math

import jax
import jax.numpy as jnp
import numpy as np
from jax import lax
from jax.experimental import pallas as pl
from jax.experimental.pallas import tpu as pltpu
from jax.sharding import PartitionSpec as P

F32 = jnp.float32
BF16 = jnp.bfloat16
MESH = pl.DeviceIdType.MESH

KWAVE = 20.0
DELTA = 0.25
GOLDEN = math.pi * (3.0 - math.sqrt(5.0))
TURN = KWAVE / (2.0 * math.pi)
SOFT = DELTA * DELTA * TURN * TURN
Q0 = -1.03910273
P0, P1, P2 = -0.33076115, 1.40669993, -0.3346358

TILE = 512
ROWS = 64
BLOCK = 16
NT = (((1,), (1,)), ((), ()))
TN = (((0,), (0,)), ((), ()))


def half_angle(t):
    f = t - jnp.round(t)
    u = f * f
    return (P2 * u + P1) * u + P0, f * (u + Q0)


def rotated(x, axis):
    half = x.shape[axis] // 2
    re = lax.slice_in_dim(x, 0, half, axis=axis)
    im = lax.slice_in_dim(x, half, 2 * half, axis=axis)
    return jnp.concatenate((-im, re), axis)


def lane_rotated(x):
    half = x.shape[-1] // 2
    lane = lax.broadcasted_iota(jnp.int32, x.shape, x.ndim - 1)
    turned = pltpu.roll(x, half, x.ndim - 1)
    return jnp.where(lane < half, -turned, turned)


def remote(src, dst, send_sem, recv_sem, device):
    return pltpu.make_async_remote_copy(
        src_ref=src,
        dst_ref=dst,
        send_sem=send_sem,
        recv_sem=recv_sem,
        device_id=device,
        device_id_type=MESH,
    )


def product_kernel(
    n_grp, n_sub,
    vec_in, geo_in, tran_in, dirs_in,
    applied, gram,
    vec, geo_raw, tran, dirs, geo, wv, wv_nb, geo_nb, tables, moment, mom_recv, grp_src, grp_recv, tran_t, loc, loc_mat,
    xrep, yrep, g, acc, z_acc, z_send, z_recv,
    gram_src, gram_recv, gsum_recv, gram_all,
    halo_s, halo_r, mom_s, mom_r, grp_s, grp_r, loc_s, loc_r, z_s, z_r,
    gr_s, gr_r, gg_s, gg_r, ga_s, ga_r, in_s,
):
    loads = [
        pltpu.make_async_copy(src, dst, in_s.at[n])
        for n, (src, dst) in enumerate(
            ((geo_in, geo_raw), (dirs_in, dirs), (vec_in, vec), (tran_in, tran))
        )
    ]
    for load in loads:
        load.start()
    cols, panels = vec.shape
    dir_count = dirs.shape[0]
    chunk = dir_count // n_sub
    n_tiles = panels // TILE
    me_s = lax.axis_index("sub")
    me_g = lax.axis_index("grp")
    has_right = me_s < n_sub - 1
    has_left = me_s > 0

    def peer(k):
        return lax.rem(me_s + k, n_sub)

    def peer_g(k):
        return lax.rem(me_g + k, n_grp)

    barrier = pltpu.get_barrier_semaphore()

    def greet(k, _):
        pl.semaphore_signal(barrier, inc=1, device_id={"sub": peer(k)}, device_id_type=MESH)
        return 0

    lax.fori_loop(1, n_sub, greet, 0)

    def greet_g(k, _):
        pl.semaphore_signal(barrier, inc=1, device_id={"grp": peer_g(k)}, device_id_type=MESH)
        return 0

    lax.fori_loop(1, n_grp, greet_g, 0)

    for load in loads[:2]:
        load.wait()
    raw = geo_raw[...].astype(F32)
    geo[...] = jnp.concatenate((raw,) * 4, 0).astype(BF16)

    def halo(dst_sub):
        return (
            remote(wv, wv_nb, halo_s.at[0], halo_r.at[0], {"sub": dst_sub}),
            remote(geo, geo_nb, halo_s.at[1], halo_r.at[1], {"sub": dst_sub}),
        )

    left = lax.rem(me_s + n_sub - 1, n_sub)
    right = lax.rem(me_s + 1, n_sub)

    half = panels // 2

    def far_tables(n, _):
        k = n // 2
        col = pl.multiple_of((n % 2) * half, half)
        turns = jnp.dot(
            dirs[pl.ds(pl.multiple_of(k * 128, 128), 128), :],
            geo[:, pl.ds(col, half)],
            preferred_element_type=F32,
        )
        a, b = half_angle(turns)
        aa, bb = a * a, b * b
        norm = aa + bb
        inv = lax.rsqrt(norm * norm)
        row = pl.multiple_of(k * 256, 256)
        tables[pl.ds(row, 128), pl.ds(col, half)] = ((aa - bb) * inv).astype(BF16)
        tables[pl.ds(row + 128, 128), pl.ds(col, half)] = (a * b * inv).astype(BF16)
        return 0

    lax.fori_loop(0, dir_count // 128 * 2, far_tables, 0)

    for load in loads[2:]:
        load.wait()
    weight = geo[3:4, :].astype(F32)
    wv[...] = (vec[...].astype(F32) * weight).astype(BF16)

    pl.semaphore_wait(barrier, n_sub - 1 + n_grp - 1)

    @pl.when(has_left)
    def _():
        for copy in halo(left):
            copy.start()

    moment_scale = (panels * n_sub) ** (-0.5)
    for k in range(dir_count // 128):
        both = lax.dot_general(
            tables[k * 256 : k * 256 + 256, :], wv[...], NT, preferred_element_type=F32
        )
        moment[k * 128 : k * 128 + 128, :] = (
            both[:128] - 2.0 * lane_rotated(both[128:])
        ) * moment_scale

    def rows_of(ref, i, size):
        return ref.at[pl.ds(pl.multiple_of(i * size, size), size), :]

    def send_moment(k, _):
        p = peer(k)
        remote(
            rows_of(moment, p, chunk), mom_recv.at[me_s], mom_s.at[0], mom_r.at[0], {"sub": p}
        ).start()
        return 0

    lax.fori_loop(1, n_sub, send_moment, 0)

    for k in range(3):
        xrep[k] = jnp.broadcast_to(geo[k : k + 1, :].astype(F32) * TURN, (8, panels))

    def source_side(geo_ref, base, offset):
        rows = lax.broadcasted_iota(jnp.int32, (16, 3 * 128), 0)
        lanes = lax.broadcasted_iota(jnp.int32, (16, 3 * 128), 1)
        pick = (lanes >= rows * 128) & (lanes < rows * 128 + 128)
        sel = jnp.where(pick, 1.0, 0.0).astype(BF16)

        for col in range(0, panels, TILE):
            y = lax.dot_general(
                geo_ref[:, col : col + TILE], sel, TN, preferred_element_type=F32
            )
            for k in range(3):
                part = y[:, k * 128 : k * 128 + 128]
                if k == 0 and offset:
                    part = part + float(offset)
                yrep[k, base + col : base + col + TILE, :] = part * TURN

    source_side(geo, 0, 0)
    acc[...] = jnp.zeros_like(acc)

    def near_tile(source, target, weighted, mirror):
        i0 = pl.multiple_of(target * TILE, TILE)

        def strip(r, _):
            for l in range(0, TILE, 128):
                for sub in range(0, ROWS, 16):
                    row = pl.multiple_of(source * TILE + r * ROWS, ROWS) + sub

                    def diff(k):
                        y = yrep[k, pl.ds(row, 16), :].reshape(2, 8, 128)
                        return xrep[k, :, pl.ds(pl.multiple_of(i0 + l, 128), 128)] - y

                    dx, dy, dz = diff(0), diff(1), diff(2)
                    d2 = dx * dx + dy * dy + dz * dz
                    d2e = d2 + 1e-30
                    a, b = half_angle(d2e * lax.rsqrt(d2e))
                    aa, bb = a * a, b * b
                    norm = aa + bb
                    inv = lax.rsqrt(norm * norm * (d2 + SOFT))
                    at = pl.multiple_of(r * ROWS, ROWS) + sub
                    g[pl.ds(at, 16), l : l + 128] = (
                        ((aa - bb) * inv).reshape(16, 128).astype(BF16)
                    )
                    g[pl.ds(at + TILE, 16), l : l + 128] = (
                        ((a * b) * inv).reshape(16, 128).astype(BF16)
                    )
            return 0

        lax.fori_loop(0, TILE // ROWS, strip, 0)
        for part in range(2):
            acc[part * cols : part * cols + cols, pl.ds(i0, TILE)] += jnp.dot(
                weighted, g[part * TILE : part * TILE + TILE, :], preferred_element_type=F32
            )
        if mirror is not None:
            ref, at = mirror
            for part in range(2):
                ref[part * cols : part * cols + cols, at : at + TILE] += lax.dot_general(
                    wv[:, pl.ds(i0, TILE)], g[part * TILE : part * TILE + TILE, :], NT,
                    preferred_element_type=F32,
                )

    def joined(re, im):
        return re + 2.0 * rotated(im, 0)

    def send_z(j):
        return remote(z_send.at[j], z_recv.at[j], z_s.at[j], z_r.at[j], {"sub": right})

    def neighbour_start():
        @pl.when(has_right)
        def _():
            for copy in halo(left):
                copy.wait_recv()
            source_side(geo_nb, panels, 1)

    def neighbour_block(j):
        @pl.when(has_right)
        def _():
            z_acc[...] = jnp.zeros_like(z_acc)

            def step(i, _):
                near_tile(n_tiles + j, i, wv_nb[:, j * TILE : j * TILE + TILE], (z_acc, 0))
                return 0

            lax.fori_loop(0, n_tiles, step, 0)
            z_send[j] = joined(z_acc[:cols], z_acc[cols:]).astype(BF16)
            send_z(j).start()

    def own_block(j):
        weighted = wv[:, j * TILE : j * TILE + TILE]
        near_tile(j, j, weighted, None)
        if j < n_tiles - 1:

            def step(i, _):
                near_tile(j, i, weighted, (acc, j * TILE))
                return 0

            lax.fori_loop(j + 1, n_tiles, step, 0)

    def reduce_moment():
        rest = mom_recv.at[pl.ds(0, n_sub - 1)]
        remote(rest, rest, mom_s.at[0], mom_r.at[0], {"sub": right}).wait()
        mom_recv[me_s] = moment[pl.ds(pl.multiple_of(me_s * chunk, chunk), chunk), :]
        total = mom_recv[0]
        for n in range(1, n_sub):
            total = total + mom_recv[n]
        grp_src[...] = total
        grp_recv[me_g] = total

        def send(k, _):
            p = peer_g(k)
            remote(grp_src, grp_recv.at[me_g], grp_s.at[p], grp_r.at[me_g], {"grp": p}).start()
            return 0

        lax.fori_loop(1, n_grp, send, 0)

    def translate():
        def arrived(k, _):
            p = peer_g(k)
            remote(grp_src, grp_recv.at[p], grp_s.at[p], grp_r.at[p], {"grp": p}).wait()
            return 0

        lax.fori_loop(1, n_grp, arrived, 0)
        for part in range(2):
            tran_t[:, part * n_grp : part * n_grp + n_grp] = tran[part, 0].T
        coef = tran_t[pl.ds(pl.multiple_of(me_s * chunk, chunk), chunk), :]
        total = jnp.zeros((chunk, cols), F32)
        for h in range(n_grp):
            m = grp_recv[h]
            total = total + coef[:, h : h + 1] * m
            total = total + coef[:, n_grp + h : n_grp + h + 1] * lane_rotated(m)
        loc[me_s] = total.astype(BF16)

        def send(k, _):
            p = peer(k)
            remote(loc.at[me_s], loc.at[me_s], loc_s.at[0], loc_r.at[0], {"sub": p}).start()
            return 0

        lax.fori_loop(1, n_sub, send, 0)

    own_block(0)
    own_block(1)
    neighbour_start()
    neighbour_block(0)
    reduce_moment()
    neighbour_block(1)
    translate()
    for j in range(2, n_tiles):
        neighbour_block(j)
    for j in range(2, n_tiles):
        own_block(j)

    rest = loc.at[pl.ds(0, n_sub - 1)]
    remote(rest, rest, loc_s.at[0], loc_r.at[0], {"sub": right}).wait()
    per = 128 // chunk
    for k in range(dir_count // 128):
        block = jnp.concatenate([loc[k * per + n].astype(F32) for n in range(per)], 0)
        loc_mat[:, k * 256 : k * 256 + 128] = block.T.astype(BF16)
        loc_mat[:, k * 256 + 128 : k * 256 + 256] = (2.0 * lane_rotated(block)).T.astype(BF16)

    @pl.when(has_left)
    def _():
        for copy in halo(left):
            copy.wait_send()
        for j in range(n_tiles):
            send_z(j).wait_recv()
            acc[:cols, j * TILE : j * TILE + TILE] += z_recv[j].astype(F32)

    @pl.when(has_right)
    def _():
        for j in range(n_tiles):
            send_z(j).wait_send()

    near_scale = TURN * (3 * panels) ** (-0.5)
    far_scale = (dir_count * n_grp) ** (-0.5)
    partial = jnp.zeros((cols, cols), F32)
    for j in range(n_tiles):
        at = slice(j * TILE, j * TILE + TILE)
        far = jnp.dot(loc_mat[...], tables[:, at], preferred_element_type=F32)
        tile = (
            0.5 * vec[:, at].astype(F32) + near_scale * joined(acc[:cols, at], acc[cols:, at]) + far_scale * far
        ).astype(BF16)
        applied[:, at] = tile
        partial = partial + lax.dot_general(tile, tile, NT, preferred_element_type=F32)
    partial = partial * (1.0 / (panels * n_sub * n_grp))

    n_own = cols // 8
    stride = n_sub // n_own
    mine = me_s // stride
    owner = lax.rem(me_s, stride) == 0
    gram_src[...] = partial.reshape(n_own, 8, cols)

    def send_block(c):
        remote(
            gram_src.at[c], gram_recv.at[me_s], gr_s.at[0], gr_r.at[0], {"sub": c * stride}
        ).start()

    def wait_for(ref, count, send_sem, recv_sem):
        part = ref.at[pl.ds(0, count)]
        return remote(part, part, send_sem.at[0], recv_sem.at[0], {"sub": right})

    def send_gram(k, _):
        send_block(lax.rem(mine + k, n_own))
        return 0

    lax.fori_loop(1, n_own, send_gram, 0)

    @pl.when(jnp.logical_not(owner))
    def _():
        send_block(mine)

    @pl.when(owner)
    def _():
        wait_for(gram_recv, n_sub - 1, gr_s, gr_r).wait_recv()
        gram_recv[me_s] = gram_src[mine]
        total = gram_recv[0]
        for n in range(1, n_sub):
            total = total + gram_recv[n]
        gsum_recv[me_g] = total

        def swap(k):
            p = peer_g(k)
            return remote(
                gsum_recv.at[me_g], gsum_recv.at[me_g], gg_s.at[p], gg_r.at[me_g], {"grp": p}
            )

        def swapped(k):
            p = peer_g(k)
            return remote(
                gsum_recv.at[me_g], gsum_recv.at[p], gg_s.at[p], gg_r.at[p], {"grp": p}
            )

        for k in range(1, n_grp):
            swap(k).start()
        for k in range(1, n_grp):
            swapped(k).wait_recv()
        total = gsum_recv[0]
        for n in range(1, n_grp):
            total = total + gsum_recv[n]
        gram_all[mine] = total

        def spread(k, _):
            remote(
                gram_all.at[mine], gram_all.at[mine], ga_s.at[0], ga_r.at[0], {"sub": peer(k)}
            ).start()
            return 0

        lax.fori_loop(1, n_sub, spread, 0)
        for k in range(1, n_grp):
            swap(k).wait_send()
        wait_for(gram_src, n_own - 1, gr_s, gr_r).wait_send()
        wait_for(gram_all, n_own - 1, ga_s, ga_r).wait_recv()

    @pl.when(jnp.logical_not(owner))
    def _():
        wait_for(gram_src, n_own, gr_s, gr_r).wait_send()
        wait_for(gram_all, n_own, ga_s, ga_r).wait_recv()

    gram[...] = gram_all[...].reshape(cols, cols)

    @pl.when(owner)
    def _():
        wait_for(gram_recv, n_sub - 1, ga_s, ga_r).wait_send()


def factor_kernel(gram, applied_in, ortho, upper, work, inverse, applied, sems):
    n = gram.shape[0]
    load_gram = pltpu.make_async_copy(gram, work, sems.at[0])
    load_applied = pltpu.make_async_copy(applied_in, applied, sems.at[1])
    load_gram.start()
    load_applied.start()
    load_gram.wait()
    sub = lax.broadcasted_iota(jnp.int32, (BLOCK, n), 0)
    lane = lax.broadcasted_iota(jnp.int32, (BLOCK, n), 1)
    for k in range(0, n, BLOCK):
        rows = work[k : k + BLOCK, :]
        col = [jnp.broadcast_to(rows[:, k + j : k + j + 1], (BLOCK, n)) for j in range(BLOCK)]
        inside = (lane >= k) & (lane < k + BLOCK)
        panel = jnp.where(inside, jnp.where(lane - k == sub, 1.0, 0.0), rows)
        scale = jnp.ones((BLOCK, n), F32)
        for j in range(BLOCK):
            root = lax.rsqrt(jnp.broadcast_to(col[j][j : j + 1, :], (BLOCK, n)))
            scale = jnp.where(sub == j, root, scale)
            if j < BLOCK - 1:
                ratio = jnp.where(sub > j, col[j] * (root * root), 0.0)
                for l in range(j + 1, BLOCK):
                    col[l] = col[l] - ratio * jnp.broadcast_to(col[l][j : j + 1, :], (BLOCK, n))
                panel = panel - ratio * jnp.broadcast_to(panel[j : j + 1, :], (BLOCK, n))
        panel = panel * scale
        inverse[k : k + BLOCK, :] = jnp.where(lane < k + BLOCK, panel, 0.0)
        corner = jnp.zeros((BLOCK, n), F32)
        for j in range(BLOCK):
            corner = jnp.where((lane == k + j) & (sub <= j), col[j], corner)
        upper[k : k + BLOCK, :] = jnp.where(lane >= k + BLOCK, panel, corner * scale)
        if k + BLOCK < n:
            hi = panel.astype(BF16).astype(F32)
            rest = panel - hi
            mid = rest.astype(BF16).astype(F32)
            lo = rest - mid
            left = jnp.concatenate((hi, hi, mid, hi, lo, mid), 0).astype(BF16)
            right = jnp.concatenate((hi, mid, hi, lo, hi, mid), 0).astype(BF16)
            update = lax.dot_general(left, right, TN, preferred_element_type=F32)
            below = work[k + BLOCK :, :]
            at = lax.broadcasted_iota(jnp.int32, below.shape, 1)
            below = jnp.where((at >= k) & (at < k + BLOCK), 0.0, below)
            work[k + BLOCK :, :] = below - update[k + BLOCK :, :]
    load_applied.wait()
    whole = inverse[...]
    hi = whole.astype(BF16)
    lo = (whole - hi.astype(F32)).astype(BF16)
    for c in range(0, applied.shape[1], TILE):
        tile = applied[:, c : c + TILE]
        ortho[:, c : c + TILE] = jnp.dot(hi, tile, preferred_element_type=F32) + jnp.dot(
            lo, tile, preferred_element_type=F32
        )


def direction_table(count):
    serial = np.arange(count).astype(np.float32)
    height = (1.0 - (2.0 * serial.astype(np.float64) + 1.0) / count)
    radius = np.sqrt(np.maximum(1.0 - height * height, 0.0))
    azimuth = (serial * np.float32(GOLDEN)).astype(np.float64)
    unit = TURN * np.stack((radius * np.cos(azimuth), radius * np.sin(azimuth), height), 1)
    table = np.zeros((count, 16), np.float64)
    for part in range(3):
        piece = unit.astype(jnp.bfloat16).astype(np.float64)
        table[:, 4 * part : 4 * part + 3] = piece
        unit = unit - piece
    return table.astype(jnp.bfloat16)


def shards(n_grp, n_sub, vectors, geometry, transfer):
    cols, panels = vectors.shape
    dir_count = transfer.shape[-1]
    chunk = dir_count // n_sub
    n_tiles = panels // TILE
    n_own = cols // 8
    dma = pltpu.SemaphoreType.DMA
    applied, gram = pl.pallas_call(
        functools.partial(product_kernel, n_grp, n_sub),
        out_shape=(
            jax.ShapeDtypeStruct((cols, panels), BF16),
            jax.ShapeDtypeStruct((cols, cols), F32),
        ),
        in_specs=[pl.BlockSpec(memory_space=pl.ANY)] * 4,
        out_specs=[pl.BlockSpec(memory_space=pltpu.VMEM)] * 2,
        scratch_shapes=[
            pltpu.VMEM((cols, panels), BF16),
            pltpu.VMEM((4, panels), BF16),
            pltpu.VMEM(transfer.shape, F32),
            pltpu.VMEM((dir_count, 16), BF16),
            pltpu.VMEM((16, panels), BF16),
            pltpu.VMEM((cols, panels), BF16),
            pltpu.VMEM((cols, panels), BF16),
            pltpu.VMEM((16, panels), BF16),
            pltpu.VMEM((2 * dir_count, panels), BF16),
            pltpu.VMEM((dir_count, cols), F32),
            pltpu.VMEM((n_sub, chunk, cols), F32),
            pltpu.VMEM((chunk, cols), F32),
            pltpu.VMEM((n_grp, chunk, cols), F32),
            pltpu.VMEM((dir_count, 2 * n_grp), F32),
            pltpu.VMEM((n_sub, chunk, cols), BF16),
            pltpu.VMEM((cols, 2 * dir_count), BF16),
            pltpu.VMEM((3, 8, panels), F32),
            pltpu.VMEM((3, 2 * panels, 128), F32),
            pltpu.VMEM((2 * TILE, TILE), BF16),
            pltpu.VMEM((2 * cols, panels), F32),
            pltpu.VMEM((2 * cols, TILE), F32),
            pltpu.VMEM((n_tiles, cols, TILE), BF16),
            pltpu.VMEM((n_tiles, cols, TILE), BF16),
            pltpu.VMEM((n_own, 8, cols), F32),
            pltpu.VMEM((n_sub, 8, cols), F32),
            pltpu.VMEM((n_grp, 8, cols), F32),
            pltpu.VMEM((n_own, 8, cols), F32),
            dma((2,)), dma((2,)),
            dma((1,)), dma((1,)),
            dma((n_grp,)), dma((n_grp,)),
            dma((1,)), dma((1,)),
            dma((n_tiles,)), dma((n_tiles,)),
            dma((1,)), dma((1,)),
            dma((n_grp,)), dma((n_grp,)),
            dma((1,)), dma((1,)),
            dma((4,)),
        ],
        compiler_params=pltpu.CompilerParams(
            collective_id=0, has_side_effects=True, vmem_limit_bytes=56 << 20
        ),
    )(vectors, geometry, transfer, jnp.asarray(direction_table(dir_count)))
    return tuple(
        pl.pallas_call(
            factor_kernel,
            out_shape=(
                jax.ShapeDtypeStruct((cols, panels), F32),
                jax.ShapeDtypeStruct((cols, cols), F32),
            ),
            in_specs=[pl.BlockSpec(memory_space=pl.ANY)] * 2,
            out_specs=[pl.BlockSpec(memory_space=pltpu.VMEM)] * 2,
            scratch_shapes=[
                pltpu.VMEM((cols, cols), F32),
                pltpu.VMEM((cols, cols), F32),
                pltpu.VMEM((cols, panels), BF16),
                dma((2,)),
            ],
            compiler_params=pltpu.CompilerParams(vmem_limit_bytes=56 << 20),
        )(gram, applied)
    )


def solution(mesh):
    in_specs = (P(None, ("grp", "sub")), P(None, ("grp", "sub")), P(None, "grp", None, None))
    out_specs = (P(None, ("grp", "sub")), P())
    body = functools.partial(shards, mesh.shape["grp"], mesh.shape["sub"])
    return jax.shard_map(body, mesh=mesh, in_specs=in_specs, out_specs=out_specs, check_vma=False)
```

```python
import functools
import math

import jax
import jax.numpy as jnp
import numpy as np
from jax import lax
from jax.experimental import pallas as pl
from jax.experimental.pallas import tpu as pltpu
from jax.sharding import PartitionSpec as P

F32 = jnp.float32
BF16 = jnp.bfloat16
MESH = pl.DeviceIdType.MESH

KWAVE = 20.0
DELTA = 0.25
GOLDEN = math.pi * (3.0 - math.sqrt(5.0))
TURN = KWAVE / (2.0 * math.pi)
SOFT = DELTA * DELTA * TURN * TURN
Q0 = -1.03910273
P0, P1, P2 = -0.33076115, 1.40669993, -0.3346358

TILE = 512
ROWS = 64
BLOCK = 16
NT = (((1,), (1,)), ((), ()))
TN = (((0,), (0,)), ((), ()))


def half_angle(t):
    f = t - jnp.round(t)
    u = f * f
    return (P2 * u + P1) * u + P0, f * (u + Q0)


def rotated(x, axis):
    half = x.shape[axis] // 2
    re = lax.slice_in_dim(x, 0, half, axis=axis)
    im = lax.slice_in_dim(x, half, 2 * half, axis=axis)
    return jnp.concatenate((-im, re), axis)


def lane_rotated(x):
    half = x.shape[-1] // 2
    lane = lax.broadcasted_iota(jnp.int32, x.shape, x.ndim - 1)
    turned = pltpu.roll(x, half, x.ndim - 1)
    return jnp.where(lane < half, -turned, turned)


def remote(src, dst, send_sem, recv_sem, device):
    return pltpu.make_async_remote_copy(
        src_ref=src,
        dst_ref=dst,
        send_sem=send_sem,
        recv_sem=recv_sem,
        device_id=device,
        device_id_type=MESH,
    )


def product_kernel(
    n_grp, n_sub,
    vec_in, geo_in, tran_in, dirs_in,
    applied_out, gram,
    vec, geo_raw, tran, dirs, geo, wv, wv_nb, geo_nb, tables, moment, mom_recv, grp_src, grp_recv, tran_t, loc, loc_mat,
    xrep, yrep, g, acc, z_acc, z_send, z_recv,
    gram_src, gram_recv, gsum_recv, gram_all,
    halo_s, halo_r, mom_s, mom_r, grp_s, grp_r, loc_s, loc_r, z_s, z_r,
    gr_s, gr_r, gg_s, gg_r, ga_s, ga_r, in_s, applied, out_s,
):
    loads = [
        pltpu.make_async_copy(src, dst, in_s.at[n])
        for n, (src, dst) in enumerate(
            ((geo_in, geo_raw), (dirs_in, dirs), (vec_in, vec), (tran_in, tran))
        )
    ]
    for load in loads:
        load.start()
    cols, panels = vec.shape
    dir_count = dirs.shape[0]
    chunk = dir_count // n_sub
    n_tiles = panels // TILE
    me_s = lax.axis_index("sub")
    me_g = lax.axis_index("grp")
    has_right = me_s < n_sub - 1
    has_left = me_s > 0

    def peer(k):
        return lax.rem(me_s + k, n_sub)

    def peer_g(k):
        return lax.rem(me_g + k, n_grp)

    barrier = pltpu.get_barrier_semaphore()

    def greet(k, _):
        pl.semaphore_signal(barrier, inc=1, device_id={"sub": peer(k)}, device_id_type=MESH)
        return 0

    lax.fori_loop(1, n_sub, greet, 0)

    def greet_g(k, _):
        pl.semaphore_signal(barrier, inc=1, device_id={"grp": peer_g(k)}, device_id_type=MESH)
        return 0

    lax.fori_loop(1, n_grp, greet_g, 0)

    for load in loads[:2]:
        load.wait()
    raw = geo_raw[...].astype(F32)
    geo[...] = jnp.concatenate((raw,) * 4, 0).astype(BF16)

    def halo(dst_sub):
        return (
            remote(wv, wv_nb, halo_s.at[0], halo_r.at[0], {"sub": dst_sub}),
            remote(geo, geo_nb, halo_s.at[1], halo_r.at[1], {"sub": dst_sub}),
        )

    left = lax.rem(me_s + n_sub - 1, n_sub)
    right = lax.rem(me_s + 1, n_sub)

    half = panels // 2

    def far_tables(n, _):
        k = n // 2
        col = pl.multiple_of((n % 2) * half, half)
        turns = jnp.dot(
            dirs[pl.ds(pl.multiple_of(k * 128, 128), 128), :],
            geo[:, pl.ds(col, half)],
            preferred_element_type=F32,
        )
        a, b = half_angle(turns)
        aa, bb = a * a, b * b
        norm = aa + bb
        inv = lax.rsqrt(norm * norm)
        row = pl.multiple_of(k * 256, 256)
        tables[pl.ds(row, 128), pl.ds(col, half)] = ((aa - bb) * inv).astype(BF16)
        tables[pl.ds(row + 128, 128), pl.ds(col, half)] = (a * b * inv).astype(BF16)
        return 0

    lax.fori_loop(0, dir_count // 128 * 2, far_tables, 0)

    for load in loads[2:]:
        load.wait()
    weight = geo[3:4, :].astype(F32)
    wv[...] = (vec[...].astype(F32) * weight).astype(BF16)

    pl.semaphore_wait(barrier, n_sub - 1 + n_grp - 1)

    @pl.when(has_left)
    def _():
        for copy in halo(left):
            copy.start()

    moment_scale = (panels * n_sub) ** (-0.5)
    for k in range(dir_count // 128):
        both = lax.dot_general(
            tables[k * 256 : k * 256 + 256, :], wv[...], NT, preferred_element_type=F32
        )
        moment[k * 128 : k * 128 + 128, :] = (
            both[:128] - 2.0 * lane_rotated(both[128:])
        ) * moment_scale

    def rows_of(ref, i, size):
        return ref.at[pl.ds(pl.multiple_of(i * size, size), size), :]

    def send_moment(k):
        p = peer(k)
        remote(
            rows_of(moment, p, chunk), mom_recv.at[me_s], mom_s.at[0], mom_r.at[0], {"sub": p}
        ).start()


    for k in range(3):
        xrep[k] = jnp.broadcast_to(geo[k : k + 1, :].astype(F32) * TURN, (8, panels))

    def source_side(geo_ref, base, offset):
        rows = lax.broadcasted_iota(jnp.int32, (16, 3 * 128), 0)
        lanes = lax.broadcasted_iota(jnp.int32, (16, 3 * 128), 1)
        pick = (lanes >= rows * 128) & (lanes < rows * 128 + 128)
        sel = jnp.where(pick, 1.0, 0.0).astype(BF16)

        for col in range(0, panels, TILE):
            y = lax.dot_general(
                geo_ref[:, col : col + TILE], sel, TN, preferred_element_type=F32
            )
            for k in range(3):
                part = y[:, k * 128 : k * 128 + 128]
                if k == 0 and offset:
                    part = part + float(offset)
                yrep[k, base + col : base + col + TILE, :] = part * TURN

    source_side(geo, 0, 0)
    acc[...] = jnp.zeros_like(acc)

    def near_tile(source, target, weighted, mirror, send=None):
        i0 = pl.multiple_of(target * TILE, TILE)

        def strip(first, r, _):
            if send is not None:
                k = target * (TILE // ROWS) + r

                @pl.when(k > 0)
                def _():
                    send(k)

            for l in range(first, TILE, 128):
                for sub in range(0, ROWS, 16):
                    row = pl.multiple_of(source * TILE + r * ROWS, ROWS) + sub

                    def diff(k):
                        y = yrep[k, pl.ds(row, 16), :].reshape(2, 8, 128)
                        return xrep[k, :, pl.ds(pl.multiple_of(i0 + l, 128), 128)] - y

                    dx, dy, dz = diff(0), diff(1), diff(2)
                    d2 = dx * dx + dy * dy + dz * dz
                    d2e = d2 + 1e-30
                    a, b = half_angle(d2e * lax.rsqrt(d2e))
                    aa, bb = a * a, b * b
                    norm = aa + bb
                    inv = lax.rsqrt(norm * norm * (d2 + SOFT))
                    at = pl.multiple_of(r * ROWS, ROWS) + sub
                    g[pl.ds(at, 16), l : l + 128] = (
                        ((aa - bb) * inv).reshape(16, 128).astype(BF16)
                    )
                    g[pl.ds(at + TILE, 16), l : l + 128] = (
                        ((a * b) * inv).reshape(16, 128).astype(BF16)
                    )
            return 0

        strips = TILE // ROWS
        if mirror is None:
            half = TILE // 2
            lax.fori_loop(0, strips // 2, functools.partial(strip, 0), 0)
            lax.fori_loop(strips // 2, strips, functools.partial(strip, half), 0)
            for part in range(2):
                at = slice(part * cols, part * cols + cols)
                upper = slice(part * TILE, part * TILE + half)
                near, far = pl.ds(i0, half), pl.ds(i0 + half, half)
                acc[at, near] += jnp.dot(
                    weighted[:, :half], g[upper, :half], preferred_element_type=F32
                ) + lax.dot_general(
                    wv[:, far], g[upper, half:], NT, preferred_element_type=F32
                )
                acc[at, far] += jnp.dot(
                    weighted, g[part * TILE : part * TILE + TILE, half:],
                    preferred_element_type=F32,
                )
            return
        lax.fori_loop(0, strips, functools.partial(strip, 0), 0)
        for part in range(2):
            acc[part * cols : part * cols + cols, pl.ds(i0, TILE)] += jnp.dot(
                weighted, g[part * TILE : part * TILE + TILE, :], preferred_element_type=F32
            )
        ref, at = mirror
        for part in range(2):
            ref[part * cols : part * cols + cols, at : at + TILE] += lax.dot_general(
                wv[:, pl.ds(i0, TILE)], g[part * TILE : part * TILE + TILE, :], NT,
                preferred_element_type=F32,
            )

    def joined(re, im):
        return re + 2.0 * rotated(im, 0)

    def send_z(j):
        return remote(z_send.at[j], z_recv.at[j], z_s.at[j], z_r.at[j], {"sub": right})

    def neighbour_start():
        @pl.when(has_right)
        def _():
            for copy in halo(left):
                copy.wait_recv()
            source_side(geo_nb, panels, 1)

    def neighbour_block(j, send=None):
        @pl.when(has_right)
        def _():
            z_acc[...] = jnp.zeros_like(z_acc)

            def step(i, _):
                near_tile(
                    n_tiles + j, i, wv_nb[:, j * TILE : j * TILE + TILE], (z_acc, 0), send
                )
                return 0

            lax.fori_loop(0, n_tiles, step, 0)
            z_send[j] = joined(z_acc[:cols], z_acc[cols:]).astype(BF16)
            send_z(j).start()

    def own_block(j, send=None):
        weighted = wv[:, j * TILE : j * TILE + TILE]
        near_tile(j, j, weighted, None, send)
        if j < n_tiles - 1:

            def step(i, _):
                near_tile(j, i, weighted, (acc, j * TILE), send)
                return 0

            lax.fori_loop(j + 1, n_tiles, step, 0)

    def reduce_moment():
        rest = mom_recv.at[pl.ds(0, n_sub - 1)]
        remote(rest, rest, mom_s.at[0], mom_r.at[0], {"sub": right}).wait()
        mom_recv[me_s] = moment[pl.ds(pl.multiple_of(me_s * chunk, chunk), chunk), :]
        total = mom_recv[0]
        for n in range(1, n_sub):
            total = total + mom_recv[n]
        grp_src[...] = total
        grp_recv[me_g] = total

        def send(k, _):
            p = peer_g(k)
            remote(grp_src, grp_recv.at[me_g], grp_s.at[p], grp_r.at[me_g], {"grp": p}).start()
            return 0

        lax.fori_loop(1, n_grp, send, 0)

    def translate():
        def arrived(k, _):
            p = peer_g(k)
            remote(grp_src, grp_recv.at[p], grp_s.at[p], grp_r.at[p], {"grp": p}).wait()
            return 0

        lax.fori_loop(1, n_grp, arrived, 0)
        for part in range(2):
            tran_t[:, part * n_grp : part * n_grp + n_grp] = tran[part, 0].T
        coef = tran_t[pl.ds(pl.multiple_of(me_s * chunk, chunk), chunk), :]
        total = jnp.zeros((chunk, cols), F32)
        for h in range(n_grp):
            m = grp_recv[h]
            total = total + coef[:, h : h + 1] * m
            total = total + coef[:, n_grp + h : n_grp + h + 1] * lane_rotated(m)
        loc[me_s] = total.astype(BF16)

    def send_local(k):
        remote(loc.at[me_s], loc.at[me_s], loc_s.at[0], loc_r.at[0], {"sub": peer(k)}).start()

    assert n_tiles * (TILE // ROWS) == n_sub
    own_block(0, send_moment)
    own_block(1)
    neighbour_start()
    neighbour_block(0)
    reduce_moment()
    neighbour_block(1)
    translate()

    @pl.when(jnp.logical_not(has_right))
    def _():
        def step(k, _):
            send_local(k)
            return 0

        lax.fori_loop(1, n_sub, step, 0)

    neighbour_block(2, send_local)
    for j in range(3, n_tiles):
        neighbour_block(j)
    for j in range(2, n_tiles):
        own_block(j)

    rest = loc.at[pl.ds(0, n_sub - 1)]
    remote(rest, rest, loc_s.at[0], loc_r.at[0], {"sub": right}).wait()
    per = 128 // chunk
    for k in range(dir_count // 128):
        block = jnp.concatenate([loc[k * per + n].astype(F32) for n in range(per)], 0)
        loc_mat[:, k * 256 : k * 256 + 128] = block.T.astype(BF16)
        loc_mat[:, k * 256 + 128 : k * 256 + 256] = (2.0 * lane_rotated(block)).T.astype(BF16)

    @pl.when(has_left)
    def _():
        for copy in halo(left):
            copy.wait_send()
        for j in range(n_tiles):
            send_z(j).wait_recv()
            acc[:cols, j * TILE : j * TILE + TILE] += z_recv[j].astype(F32)

    @pl.when(has_right)
    def _():
        for j in range(n_tiles):
            send_z(j).wait_send()

    near_scale = TURN * (3 * panels) ** (-0.5)
    far_scale = (dir_count * n_grp) ** (-0.5)
    partial = jnp.zeros((cols, cols), F32)
    for j in range(n_tiles):
        at = slice(j * TILE, j * TILE + TILE)
        far = jnp.dot(loc_mat[...], tables[:, at], preferred_element_type=F32)
        tile = (
            0.5 * vec[:, at].astype(F32) + near_scale * joined(acc[:cols, at], acc[cols:, at]) + far_scale * far
        ).astype(BF16)
        applied[:, at] = tile
        partial = partial + lax.dot_general(tile, tile, NT, preferred_element_type=F32)
    partial = partial * (1.0 / (panels * n_sub * n_grp))
    store = pltpu.make_async_copy(applied, applied_out, out_s.at[0])
    store.start()

    n_own = cols // 8
    stride = n_sub // n_own
    mine = me_s // stride
    owner = lax.rem(me_s, stride) == 0
    gram_src[...] = partial.reshape(n_own, 8, cols)

    def send_block(c):
        remote(
            gram_src.at[c], gram_recv.at[me_s], gr_s.at[0], gr_r.at[0], {"sub": c * stride}
        ).start()

    def wait_for(ref, count, send_sem, recv_sem):
        part = ref.at[pl.ds(0, count)]
        return remote(part, part, send_sem.at[0], recv_sem.at[0], {"sub": right})

    def send_gram(k, _):
        send_block(lax.rem(mine + k, n_own))
        return 0

    lax.fori_loop(1, n_own, send_gram, 0)

    @pl.when(jnp.logical_not(owner))
    def _():
        send_block(mine)

    @pl.when(owner)
    def _():
        wait_for(gram_recv, n_sub - 1, gr_s, gr_r).wait_recv()
        gram_recv[me_s] = gram_src[mine]
        total = gram_recv[0]
        for n in range(1, n_sub):
            total = total + gram_recv[n]
        gsum_recv[me_g] = total

        def swap(k):
            p = peer_g(k)
            return remote(
                gsum_recv.at[me_g], gsum_recv.at[me_g], gg_s.at[p], gg_r.at[me_g], {"grp": p}
            )

        def swapped(k):
            p = peer_g(k)
            return remote(
                gsum_recv.at[me_g], gsum_recv.at[p], gg_s.at[p], gg_r.at[p], {"grp": p}
            )

        for k in range(1, n_grp):
            swap(k).start()
        for k in range(1, n_grp):
            swapped(k).wait_recv()
        total = gsum_recv[0]
        for n in range(1, n_grp):
            total = total + gsum_recv[n]
        gram_all[mine] = total

        def spread(k, _):
            remote(
                gram_all.at[mine], gram_all.at[mine], ga_s.at[0], ga_r.at[0], {"sub": peer(k)}
            ).start()
            return 0

        lax.fori_loop(1, n_sub, spread, 0)
        for k in range(1, n_grp):
            swap(k).wait_send()
        wait_for(gram_src, n_own - 1, gr_s, gr_r).wait_send()
        wait_for(gram_all, n_own - 1, ga_s, ga_r).wait_recv()

    @pl.when(jnp.logical_not(owner))
    def _():
        wait_for(gram_src, n_own, gr_s, gr_r).wait_send()
        wait_for(gram_all, n_own, ga_s, ga_r).wait_recv()

    gram[...] = gram_all[...].reshape(cols, cols)
    store.wait()

    @pl.when(owner)
    def _():
        wait_for(gram_recv, n_sub - 1, ga_s, ga_r).wait_send()


def factor_kernel(gram, applied_in, ortho, upper, work, inverse, applied, sems):
    n = gram.shape[0]
    load_gram = pltpu.make_async_copy(gram, work, sems.at[0])
    load_applied = pltpu.make_async_copy(applied_in, applied, sems.at[1])
    load_gram.start()
    load_applied.start()
    load_gram.wait()
    sub = lax.broadcasted_iota(jnp.int32, (BLOCK, n), 0)
    lane = lax.broadcasted_iota(jnp.int32, (BLOCK, n), 1)
    for k in range(0, n, BLOCK):
        rows = work[k : k + BLOCK, :]
        col = [jnp.broadcast_to(rows[:, k + j : k + j + 1], (BLOCK, n)) for j in range(BLOCK)]
        inside = (lane >= k) & (lane < k + BLOCK)
        panel = jnp.where(inside, jnp.where(lane - k == sub, 1.0, 0.0), rows)
        scale = jnp.ones((BLOCK, n), F32)
        for j in range(BLOCK):
            root = lax.rsqrt(jnp.broadcast_to(col[j][j : j + 1, :], (BLOCK, n)))
            scale = jnp.where(sub == j, root, scale)
            if j < BLOCK - 1:
                ratio = jnp.where(sub > j, col[j] * (root * root), 0.0)
                for l in range(j + 1, BLOCK):
                    col[l] = col[l] - ratio * jnp.broadcast_to(col[l][j : j + 1, :], (BLOCK, n))
                panel = panel - ratio * jnp.broadcast_to(panel[j : j + 1, :], (BLOCK, n))
        panel = panel * scale
        inverse[k : k + BLOCK, :] = jnp.where(lane < k + BLOCK, panel, 0.0)
        corner = jnp.zeros((BLOCK, n), F32)
        for j in range(BLOCK):
            corner = jnp.where((lane == k + j) & (sub <= j), col[j], corner)
        upper[k : k + BLOCK, :] = jnp.where(lane >= k + BLOCK, panel, corner * scale)
        if k + BLOCK < n:
            hi = panel.astype(BF16).astype(F32)
            rest = panel - hi
            mid = rest.astype(BF16).astype(F32)
            lo = rest - mid
            left = jnp.concatenate((hi, hi, mid, hi, lo, mid), 0).astype(BF16)
            right = jnp.concatenate((hi, mid, hi, lo, hi, mid), 0).astype(BF16)
            update = lax.dot_general(left, right, TN, preferred_element_type=F32)
            below = work[k + BLOCK :, :]
            at = lax.broadcasted_iota(jnp.int32, below.shape, 1)
            below = jnp.where((at >= k) & (at < k + BLOCK), 0.0, below)
            work[k + BLOCK :, :] = below - update[k + BLOCK :, :]
    load_applied.wait()
    whole = inverse[...]
    hi = whole.astype(BF16)
    lo = (whole - hi.astype(F32)).astype(BF16)
    for c in range(0, applied.shape[1], TILE):
        tile = applied[:, c : c + TILE]
        ortho[:, c : c + TILE] = jnp.dot(hi, tile, preferred_element_type=F32) + jnp.dot(
            lo, tile, preferred_element_type=F32
        )


def direction_table(count):
    serial = np.arange(count).astype(np.float32)
    height = (1.0 - (2.0 * serial.astype(np.float64) + 1.0) / count)
    radius = np.sqrt(np.maximum(1.0 - height * height, 0.0))
    azimuth = (serial * np.float32(GOLDEN)).astype(np.float64)
    unit = TURN * np.stack((radius * np.cos(azimuth), radius * np.sin(azimuth), height), 1)
    table = np.zeros((count, 16), np.float64)
    for part in range(3):
        piece = unit.astype(jnp.bfloat16).astype(np.float64)
        table[:, 4 * part : 4 * part + 3] = piece
        unit = unit - piece
    return table.astype(jnp.bfloat16)


def shards(n_grp, n_sub, vectors, geometry, transfer):
    cols, panels = vectors.shape
    dir_count = transfer.shape[-1]
    chunk = dir_count // n_sub
    n_tiles = panels // TILE
    n_own = cols // 8
    dma = pltpu.SemaphoreType.DMA
    applied, gram = pl.pallas_call(
        functools.partial(product_kernel, n_grp, n_sub),
        out_shape=(
            jax.ShapeDtypeStruct((cols, panels), BF16),
            jax.ShapeDtypeStruct((cols, cols), F32),
        ),
        in_specs=[pl.BlockSpec(memory_space=pl.ANY)] * 4,
        out_specs=[
            pl.BlockSpec(memory_space=pl.ANY),
            pl.BlockSpec(memory_space=pltpu.VMEM),
        ],
        scratch_shapes=[
            pltpu.VMEM((cols, panels), BF16),
            pltpu.VMEM((4, panels), BF16),
            pltpu.VMEM(transfer.shape, F32),
            pltpu.VMEM((dir_count, 16), BF16),
            pltpu.VMEM((16, panels), BF16),
            pltpu.VMEM((cols, panels), BF16),
            pltpu.VMEM((cols, panels), BF16),
            pltpu.VMEM((16, panels), BF16),
            pltpu.VMEM((2 * dir_count, panels), BF16),
            pltpu.VMEM((dir_count, cols), F32),
            pltpu.VMEM((n_sub, chunk, cols), F32),
            pltpu.VMEM((chunk, cols), F32),
            pltpu.VMEM((n_grp, chunk, cols), F32),
            pltpu.VMEM((dir_count, 2 * n_grp), F32),
            pltpu.VMEM((n_sub, chunk, cols), BF16),
            pltpu.VMEM((cols, 2 * dir_count), BF16),
            pltpu.VMEM((3, 8, panels), F32),
            pltpu.VMEM((3, 2 * panels, 128), F32),
            pltpu.VMEM((2 * TILE, TILE), BF16),
            pltpu.VMEM((2 * cols, panels), F32),
            pltpu.VMEM((2 * cols, TILE), F32),
            pltpu.VMEM((n_tiles, cols, TILE), BF16),
            pltpu.VMEM((n_tiles, cols, TILE), BF16),
            pltpu.VMEM((n_own, 8, cols), F32),
            pltpu.VMEM((n_sub, 8, cols), F32),
            pltpu.VMEM((n_grp, 8, cols), F32),
            pltpu.VMEM((n_own, 8, cols), F32),
            dma((2,)), dma((2,)),
            dma((1,)), dma((1,)),
            dma((n_grp,)), dma((n_grp,)),
            dma((1,)), dma((1,)),
            dma((n_tiles,)), dma((n_tiles,)),
            dma((1,)), dma((1,)),
            dma((n_grp,)), dma((n_grp,)),
            dma((1,)), dma((1,)),
            dma((4,)),
            pltpu.VMEM((cols, panels), BF16),
            dma((1,)),
        ],
        compiler_params=pltpu.CompilerParams(
            collective_id=0, has_side_effects=True, vmem_limit_bytes=56 << 20
        ),
    )(vectors, geometry, transfer, jnp.asarray(direction_table(dir_count)))
    return tuple(
        pl.pallas_call(
            factor_kernel,
            out_shape=(
                jax.ShapeDtypeStruct((cols, panels), F32),
                jax.ShapeDtypeStruct((cols, cols), F32),
            ),
            in_specs=[pl.BlockSpec(memory_space=pl.ANY)] * 2,
            out_specs=[pl.BlockSpec(memory_space=pltpu.VMEM)] * 2,
            scratch_shapes=[
                pltpu.VMEM((cols, cols), F32),
                pltpu.VMEM((cols, cols), F32),
                pltpu.VMEM((cols, panels), BF16),
                dma((2,)),
            ],
            compiler_params=pltpu.CompilerParams(vmem_limit_bytes=56 << 20),
        )(gram, applied)
    )


def solution(mesh):
    in_specs = (P(None, ("grp", "sub")), P(None, ("grp", "sub")), P(None, "grp", None, None))
    out_specs = (P(None, ("grp", "sub")), P())
    body = functools.partial(shards, mesh.shape["grp"], mesh.shape["sub"])
    return jax.shard_map(body, mesh=mesh, in_specs=in_specs, out_specs=out_specs, check_vma=False)
```

```python
import functools
import math

import jax
import jax.numpy as jnp
import numpy as np
from jax import lax
from jax.experimental import pallas as pl
from jax.experimental.pallas import tpu as pltpu
from jax.sharding import PartitionSpec as P

F32 = jnp.float32
BF16 = jnp.bfloat16
MESH = pl.DeviceIdType.MESH

KWAVE = 20.0
DELTA = 0.25
GOLDEN = math.pi * (3.0 - math.sqrt(5.0))
TURN = KWAVE / (2.0 * math.pi)
SOFT = DELTA * DELTA * TURN * TURN
Q0 = -1.03910273
P0, P1, P2 = -0.33076115, 1.40669993, -0.3346358

TILE = 512
ROWS = 64
BLOCK = 16
NT = (((1,), (1,)), ((), ()))
TN = (((0,), (0,)), ((), ()))


def half_angle(t):
    f = t - jnp.round(t)
    u = f * f
    return (P2 * u + P1) * u + P0, f * (u + Q0)


def rotated(x, axis):
    half = x.shape[axis] // 2
    re = lax.slice_in_dim(x, 0, half, axis=axis)
    im = lax.slice_in_dim(x, half, 2 * half, axis=axis)
    return jnp.concatenate((-im, re), axis)


def lane_rotated(x):
    half = x.shape[-1] // 2
    lane = lax.broadcasted_iota(jnp.int32, x.shape, x.ndim - 1)
    turned = pltpu.roll(x, half, x.ndim - 1)
    return jnp.where(lane < half, -turned, turned)


def remote(src, dst, send_sem, recv_sem, device):
    return pltpu.make_async_remote_copy(
        src_ref=src,
        dst_ref=dst,
        send_sem=send_sem,
        recv_sem=recv_sem,
        device_id=device,
        device_id_type=MESH,
    )


def product_kernel(
    n_grp, n_sub,
    vec_in, geo_in, tran_in, dirs_in,
    applied_out, gram,
    vec, geo_raw, tran, dirs, geo, wv, wv_nb, geo_nb, tables, moment, mom_recv, grp_src, grp_recv, tran_t, loc, loc_mat,
    xrep, yrep, g, acc, z_acc, z_send, z_recv,
    gram_src, gram_recv, gsum_recv, gram_all,
    halo_s, halo_r, mom_s, mom_r, grp_s, grp_r, loc_s, loc_r, z_s, z_r,
    gr_s, gr_r, gg_s, gg_r, ga_s, ga_r, in_s, applied, out_s,
):
    loads = [
        pltpu.make_async_copy(src, dst, in_s.at[n])
        for n, (src, dst) in enumerate(
            ((geo_in, geo_raw), (dirs_in, dirs), (vec_in, vec), (tran_in, tran))
        )
    ]
    for load in loads:
        load.start()
    cols, panels = vec.shape
    dir_count = dirs.shape[0]
    chunk = dir_count // n_sub
    n_tiles = panels // TILE
    me_s = lax.axis_index("sub")
    me_g = lax.axis_index("grp")
    has_right = me_s < n_sub - 1
    has_left = me_s > 0

    def peer(k):
        return lax.rem(me_s + k, n_sub)

    def peer_g(k):
        return lax.rem(me_g + k, n_grp)

    barrier = pltpu.get_barrier_semaphore()

    def greet(k, _):
        pl.semaphore_signal(barrier, inc=1, device_id={"sub": peer(k)}, device_id_type=MESH)
        return 0

    lax.fori_loop(1, n_sub, greet, 0)

    def greet_g(k, _):
        pl.semaphore_signal(barrier, inc=1, device_id={"grp": peer_g(k)}, device_id_type=MESH)
        return 0

    lax.fori_loop(1, n_grp, greet_g, 0)

    for load in loads[:2]:
        load.wait()
    raw = geo_raw[...].astype(F32)
    geo[...] = jnp.concatenate((raw,) * 4, 0).astype(BF16)

    def halo(dst_sub):
        return (
            remote(wv, wv_nb, halo_s.at[0], halo_r.at[0], {"sub": dst_sub}),
            remote(geo, geo_nb, halo_s.at[1], halo_r.at[1], {"sub": dst_sub}),
        )

    left = lax.rem(me_s + n_sub - 1, n_sub)
    right = lax.rem(me_s + 1, n_sub)

    half = panels // 2

    def far_tables(n, _):
        k = n // 2
        col = pl.multiple_of((n % 2) * half, half)
        turns = jnp.dot(
            dirs[pl.ds(pl.multiple_of(k * 128, 128), 128), :],
            geo[:, pl.ds(col, half)],
            preferred_element_type=F32,
        )
        a, b = half_angle(turns)
        aa, bb = a * a, b * b
        norm = aa + bb
        inv = lax.rsqrt(norm * norm)
        row = pl.multiple_of(k * 256, 256)
        tables[pl.ds(row, 128), pl.ds(col, half)] = ((aa - bb) * inv).astype(BF16)
        tables[pl.ds(row + 128, 128), pl.ds(col, half)] = (a * b * inv).astype(BF16)
        return 0

    lax.fori_loop(0, dir_count // 128 * 2, far_tables, 0)

    for load in loads[2:]:
        load.wait()
    weight = geo[3:4, :].astype(F32)
    wv[...] = (vec[...].astype(F32) * weight).astype(BF16)

    pl.semaphore_wait(barrier, n_sub - 1 + n_grp - 1)

    @pl.when(has_left)
    def _():
        for copy in halo(left):
            copy.start()

    moment_scale = (panels * n_sub) ** (-0.5)
    for k in range(dir_count // 128):
        both = lax.dot_general(
            tables[k * 256 : k * 256 + 256, :], wv[...], NT, preferred_element_type=F32
        )
        moment[k * 128 : k * 128 + 128, :] = (
            both[:128] - 2.0 * lane_rotated(both[128:])
        ) * moment_scale

    def rows_of(ref, i, size):
        return ref.at[pl.ds(pl.multiple_of(i * size, size), size), :]

    def send_moment(k):
        p = peer(k)
        remote(
            rows_of(moment, p, chunk), mom_recv.at[me_s], mom_s.at[0], mom_r.at[0], {"sub": p}
        ).start()


    for k in range(3):
        xrep[k] = jnp.broadcast_to(geo[k : k + 1, :].astype(F32) * TURN, (8, panels))

    def source_side(geo_ref, base, offset):
        rows = lax.broadcasted_iota(jnp.int32, (16, 3 * 128), 0)
        lanes = lax.broadcasted_iota(jnp.int32, (16, 3 * 128), 1)
        pick = (lanes >= rows * 128) & (lanes < rows * 128 + 128)
        sel = jnp.where(pick, 1.0, 0.0).astype(BF16)

        for col in range(0, panels, TILE):
            y = lax.dot_general(
                geo_ref[:, col : col + TILE], sel, TN, preferred_element_type=F32
            )
            for k in range(3):
                part = y[:, k * 128 : k * 128 + 128]
                if k == 0 and offset:
                    part = part + float(offset)
                yrep[k, base + col : base + col + TILE, :] = part * TURN

    source_side(geo, 0, 0)
    acc[...] = jnp.zeros_like(acc)

    def near_tile(source, target, weighted, mirror, send=None):
        i0 = pl.multiple_of(target * TILE, TILE)

        def strip(first, r, _):
            if send is not None:
                k = target * (TILE // ROWS) + r

                @pl.when(k > 0)
                def _():
                    send(k)

            for l in range(first, TILE, 128):
                for sub in range(0, ROWS, 16):
                    row = pl.multiple_of(source * TILE + r * ROWS, ROWS) + sub

                    def diff(k):
                        y = yrep[k, pl.ds(row, 16), :].reshape(2, 8, 128)
                        return xrep[k, :, pl.ds(pl.multiple_of(i0 + l, 128), 128)] - y

                    dx, dy, dz = diff(0), diff(1), diff(2)
                    d2 = dx * dx + dy * dy + dz * dz
                    d2e = d2 + 1e-30
                    a, b = half_angle(d2e * lax.rsqrt(d2e))
                    aa, bb = a * a, b * b
                    norm = aa + bb
                    inv = lax.rsqrt(norm * norm * (d2 + SOFT))
                    at = pl.multiple_of(r * ROWS, ROWS) + sub
                    g[pl.ds(at, 16), l : l + 128] = (
                        ((aa - bb) * inv).reshape(16, 128).astype(BF16)
                    )
                    g[pl.ds(at + TILE, 16), l : l + 128] = (
                        ((a * b) * inv).reshape(16, 128).astype(BF16)
                    )
            return 0

        strips = TILE // ROWS
        if mirror is None:
            half = TILE // 2
            lax.fori_loop(0, strips // 2, functools.partial(strip, 0), 0)
            lax.fori_loop(strips // 2, strips, functools.partial(strip, half), 0)
            for part in range(2):
                at = slice(part * cols, part * cols + cols)
                upper = slice(part * TILE, part * TILE + half)
                near, far = pl.ds(i0, half), pl.ds(i0 + half, half)
                acc[at, near] += jnp.dot(
                    weighted[:, :half], g[upper, :half], preferred_element_type=F32
                ) + lax.dot_general(
                    wv[:, far], g[upper, half:], NT, preferred_element_type=F32
                )
                acc[at, far] += jnp.dot(
                    weighted, g[part * TILE : part * TILE + TILE, half:],
                    preferred_element_type=F32,
                )
            return
        lax.fori_loop(0, strips, functools.partial(strip, 0), 0)
        for part in range(2):
            acc[part * cols : part * cols + cols, pl.ds(i0, TILE)] += jnp.dot(
                weighted, g[part * TILE : part * TILE + TILE, :], preferred_element_type=F32
            )
        ref, at = mirror
        for part in range(2):
            ref[part * cols : part * cols + cols, at : at + TILE] += lax.dot_general(
                wv[:, pl.ds(i0, TILE)], g[part * TILE : part * TILE + TILE, :], NT,
                preferred_element_type=F32,
            )

    def joined(re, im):
        return re + 2.0 * rotated(im, 0)

    def send_z(j):
        return remote(z_send.at[j], z_recv.at[j], z_s.at[j], z_r.at[j], {"sub": right})

    def neighbour_start():
        @pl.when(has_right)
        def _():
            for copy in halo(left):
                copy.wait_recv()
            source_side(geo_nb, panels, 1)

    def neighbour_block(j, send=None):
        @pl.when(has_right)
        def _():
            z_acc[...] = jnp.zeros_like(z_acc)

            def step(i, _):
                near_tile(
                    n_tiles + j, i, wv_nb[:, j * TILE : j * TILE + TILE], (z_acc, 0), send
                )
                return 0

            lax.fori_loop(0, n_tiles, step, 0)
            z_send[j] = joined(z_acc[:cols], z_acc[cols:]).astype(BF16)
            send_z(j).start()

    def own_block(j, send=None):
        weighted = wv[:, j * TILE : j * TILE + TILE]
        near_tile(j, j, weighted, None, send)
        if j < n_tiles - 1:

            def step(i, _):
                near_tile(j, i, weighted, (acc, j * TILE), send)
                return 0

            lax.fori_loop(j + 1, n_tiles, step, 0)

    def reduce_moment():
        rest = mom_recv.at[pl.ds(0, n_sub - 1)]
        remote(rest, rest, mom_s.at[0], mom_r.at[0], {"sub": right}).wait()
        mom_recv[me_s] = moment[pl.ds(pl.multiple_of(me_s * chunk, chunk), chunk), :]
        total = mom_recv[0]
        for n in range(1, n_sub):
            total = total + mom_recv[n]
        grp_src[...] = total
        grp_recv[me_g] = total

        def send(k, _):
            p = peer_g(k)
            remote(grp_src, grp_recv.at[me_g], grp_s.at[p], grp_r.at[me_g], {"grp": p}).start()
            return 0

        lax.fori_loop(1, n_grp, send, 0)

    def translate():
        def arrived(k, _):
            p = peer_g(k)
            remote(grp_src, grp_recv.at[p], grp_s.at[p], grp_r.at[p], {"grp": p}).wait()
            return 0

        lax.fori_loop(1, n_grp, arrived, 0)
        for part in range(2):
            tran_t[:, part * n_grp : part * n_grp + n_grp] = tran[part, 0].T
        coef = tran_t[pl.ds(pl.multiple_of(me_s * chunk, chunk), chunk), :]
        total = jnp.zeros((chunk, cols), F32)
        for h in range(n_grp):
            m = grp_recv[h]
            total = total + coef[:, h : h + 1] * m
            total = total + coef[:, n_grp + h : n_grp + h + 1] * lane_rotated(m)
        loc[me_s] = total.astype(BF16)

    def send_local(k):
        remote(loc.at[me_s], loc.at[me_s], loc_s.at[0], loc_r.at[0], {"sub": peer(k)}).start()

    assert n_tiles * (TILE // ROWS) == n_sub
    own_block(0, send_moment)
    own_block(1)
    neighbour_start()
    neighbour_block(0)
    reduce_moment()
    neighbour_block(1)
    translate()

    @pl.when(jnp.logical_not(has_right))
    def _():
        def step(k, _):
            send_local(k)
            return 0

        lax.fori_loop(1, n_sub, step, 0)

    neighbour_block(2, send_local)
    for j in range(3, n_tiles):
        neighbour_block(j)
    for j in range(2, n_tiles):
        own_block(j)

    rest = loc.at[pl.ds(0, n_sub - 1)]
    remote(rest, rest, loc_s.at[0], loc_r.at[0], {"sub": right}).wait()
    per = 128 // chunk
    for k in range(dir_count // 128):
        block = jnp.concatenate([loc[k * per + n].astype(F32) for n in range(per)], 0)
        loc_mat[:, k * 256 : k * 256 + 128] = block.T.astype(BF16)
        loc_mat[:, k * 256 + 128 : k * 256 + 256] = (2.0 * lane_rotated(block)).T.astype(BF16)

    @pl.when(has_left)
    def _():
        for copy in halo(left):
            copy.wait_send()
        for j in range(n_tiles):
            send_z(j).wait_recv()
            acc[:cols, j * TILE : j * TILE + TILE] += z_recv[j].astype(F32)

    @pl.when(has_right)
    def _():
        for j in range(n_tiles):
            send_z(j).wait_send()

    near_scale = TURN * (3 * panels) ** (-0.5)
    far_scale = (dir_count * n_grp) ** (-0.5)
    partial = jnp.zeros((cols, cols), F32)
    for j in range(n_tiles):
        at = slice(j * TILE, j * TILE + TILE)
        far = jnp.dot(loc_mat[...], tables[:, at], preferred_element_type=F32)
        tile = (
            0.5 * vec[:, at].astype(F32) + near_scale * joined(acc[:cols, at], acc[cols:, at]) + far_scale * far
        ).astype(BF16)
        applied[:, at] = tile
        partial = partial + lax.dot_general(tile, tile, NT, preferred_element_type=F32)
    partial = partial * (1.0 / (panels * n_sub * n_grp))
    store = pltpu.make_async_copy(applied, applied_out, out_s.at[0])
    store.start()

    n_own = cols // 8
    stride = n_sub // n_own
    mine = me_s // stride
    owner = lax.rem(me_s, stride) == 0
    gram_src[...] = partial.reshape(n_own, 8, cols)

    def send_block(c):
        remote(
            gram_src.at[c], gram_recv.at[me_s], gr_s.at[0], gr_r.at[0], {"sub": c * stride}
        ).start()

    def wait_for(ref, count, send_sem, recv_sem):
        part = ref.at[pl.ds(0, count)]
        return remote(part, part, send_sem.at[0], recv_sem.at[0], {"sub": right})

    def send_gram(k, _):
        send_block(lax.rem(mine + k, n_own))
        return 0

    lax.fori_loop(1, n_own, send_gram, 0, unroll=True)

    @pl.when(jnp.logical_not(owner))
    def _():
        send_block(mine)

    @pl.when(owner)
    def _():
        wait_for(gram_recv, n_sub - 1, gr_s, gr_r).wait_recv()
        gram_recv[me_s] = gram_src[mine]
        total = gram_recv[0]
        for n in range(1, n_sub):
            total = total + gram_recv[n]
        gsum_recv[me_g] = total

        def swap(k):
            p = peer_g(k)
            return remote(
                gsum_recv.at[me_g], gsum_recv.at[me_g], gg_s.at[p], gg_r.at[me_g], {"grp": p}
            )

        def swapped(k):
            p = peer_g(k)
            return remote(
                gsum_recv.at[me_g], gsum_recv.at[p], gg_s.at[p], gg_r.at[p], {"grp": p}
            )

        for k in range(1, n_grp):
            swap(k).start()
        for k in range(1, n_grp):
            swapped(k).wait_recv()
        total = gsum_recv[0]
        for n in range(1, n_grp):
            total = total + gsum_recv[n]
        gram_all[mine] = total

        def spread(k, _):
            remote(
                gram_all.at[mine], gram_all.at[mine], ga_s.at[0], ga_r.at[0], {"sub": peer(k)}
            ).start()
            return 0

        lax.fori_loop(1, n_sub, spread, 0, unroll=True)
        for k in range(1, n_grp):
            swap(k).wait_send()
        wait_for(gram_src, n_own - 1, gr_s, gr_r).wait_send()
        wait_for(gram_all, n_own - 1, ga_s, ga_r).wait_recv()

    @pl.when(jnp.logical_not(owner))
    def _():
        wait_for(gram_src, n_own, gr_s, gr_r).wait_send()
        wait_for(gram_all, n_own, ga_s, ga_r).wait_recv()

    gram[...] = gram_all[...].reshape(cols, cols)
    store.wait()

    @pl.when(owner)
    def _():
        wait_for(gram_recv, n_sub - 1, ga_s, ga_r).wait_send()


def factor_kernel(gram, applied_in, ortho, upper, work, inverse, applied, sems):
    n = gram.shape[0]
    load_gram = pltpu.make_async_copy(gram, work, sems.at[0])
    load_applied = pltpu.make_async_copy(applied_in, applied, sems.at[1])
    load_gram.start()
    load_applied.start()
    load_gram.wait()
    sub = lax.broadcasted_iota(jnp.int32, (BLOCK, n), 0)
    lane = lax.broadcasted_iota(jnp.int32, (BLOCK, n), 1)
    for k in range(0, n, BLOCK):
        rows = work[k : k + BLOCK, :]
        col = [jnp.broadcast_to(rows[:, k + j : k + j + 1], (BLOCK, n)) for j in range(BLOCK)]
        inside = (lane >= k) & (lane < k + BLOCK)
        panel = jnp.where(inside, jnp.where(lane - k == sub, 1.0, 0.0), rows)
        scale = jnp.ones((BLOCK, n), F32)
        for j in range(BLOCK):
            root = lax.rsqrt(jnp.broadcast_to(col[j][j : j + 1, :], (BLOCK, n)))
            scale = jnp.where(sub == j, root, scale)
            if j < BLOCK - 1:
                ratio = jnp.where(sub > j, col[j] * (root * root), 0.0)
                for l in range(j + 1, BLOCK):
                    col[l] = col[l] - ratio * jnp.broadcast_to(col[l][j : j + 1, :], (BLOCK, n))
                panel = panel - ratio * jnp.broadcast_to(panel[j : j + 1, :], (BLOCK, n))
        panel = panel * scale
        inverse[k : k + BLOCK, :] = jnp.where(lane < k + BLOCK, panel, 0.0)
        corner = jnp.zeros((BLOCK, n), F32)
        for j in range(BLOCK):
            corner = jnp.where((lane == k + j) & (sub <= j), col[j], corner)
        upper[k : k + BLOCK, :] = jnp.where(lane >= k + BLOCK, panel, corner * scale)
        if k + BLOCK < n:
            hi = panel.astype(BF16).astype(F32)
            rest = panel - hi
            mid = rest.astype(BF16).astype(F32)
            lo = rest - mid
            left = jnp.concatenate((hi, hi, mid, hi, lo, mid), 0).astype(BF16)
            right = jnp.concatenate((hi, mid, hi, lo, hi, mid), 0).astype(BF16)
            update = lax.dot_general(left, right, TN, preferred_element_type=F32)
            below = work[k + BLOCK :, :]
            at = lax.broadcasted_iota(jnp.int32, below.shape, 1)
            below = jnp.where((at >= k) & (at < k + BLOCK), 0.0, below)
            work[k + BLOCK :, :] = below - update[k + BLOCK :, :]
    load_applied.wait()
    whole = inverse[...]
    hi = whole.astype(BF16)
    lo = (whole - hi.astype(F32)).astype(BF16)
    for c in range(0, applied.shape[1], TILE):
        tile = applied[:, c : c + TILE]
        ortho[:, c : c + TILE] = jnp.dot(hi, tile, preferred_element_type=F32) + jnp.dot(
            lo, tile, preferred_element_type=F32
        )


def direction_table(count):
    serial = np.arange(count).astype(np.float32)
    height = (1.0 - (2.0 * serial.astype(np.float64) + 1.0) / count)
    radius = np.sqrt(np.maximum(1.0 - height * height, 0.0))
    azimuth = (serial * np.float32(GOLDEN)).astype(np.float64)
    unit = TURN * np.stack((radius * np.cos(azimuth), radius * np.sin(azimuth), height), 1)
    table = np.zeros((count, 16), np.float64)
    for part in range(3):
        piece = unit.astype(jnp.bfloat16).astype(np.float64)
        table[:, 4 * part : 4 * part + 3] = piece
        unit = unit - piece
    return table.astype(jnp.bfloat16)


def shards(n_grp, n_sub, vectors, geometry, transfer):
    cols, panels = vectors.shape
    dir_count = transfer.shape[-1]
    chunk = dir_count // n_sub
    n_tiles = panels // TILE
    n_own = cols // 8
    dma = pltpu.SemaphoreType.DMA
    applied, gram = pl.pallas_call(
        functools.partial(product_kernel, n_grp, n_sub),
        out_shape=(
            jax.ShapeDtypeStruct((cols, panels), BF16),
            jax.ShapeDtypeStruct((cols, cols), F32),
        ),
        in_specs=[pl.BlockSpec(memory_space=pl.ANY)] * 4,
        out_specs=[
            pl.BlockSpec(memory_space=pl.ANY),
            pl.BlockSpec(memory_space=pltpu.VMEM),
        ],
        scratch_shapes=[
            pltpu.VMEM((cols, panels), BF16),
            pltpu.VMEM((4, panels), BF16),
            pltpu.VMEM(transfer.shape, F32),
            pltpu.VMEM((dir_count, 16), BF16),
            pltpu.VMEM((16, panels), BF16),
            pltpu.VMEM((cols, panels), BF16),
            pltpu.VMEM((cols, panels), BF16),
            pltpu.VMEM((16, panels), BF16),
            pltpu.VMEM((2 * dir_count, panels), BF16),
            pltpu.VMEM((dir_count, cols), F32),
            pltpu.VMEM((n_sub, chunk, cols), F32),
            pltpu.VMEM((chunk, cols), F32),
            pltpu.VMEM((n_grp, chunk, cols), F32),
            pltpu.VMEM((dir_count, 2 * n_grp), F32),
            pltpu.VMEM((n_sub, chunk, cols), BF16),
            pltpu.VMEM((cols, 2 * dir_count), BF16),
            pltpu.VMEM((3, 8, panels), F32),
            pltpu.VMEM((3, 2 * panels, 128), F32),
            pltpu.VMEM((2 * TILE, TILE), BF16),
            pltpu.VMEM((2 * cols, panels), F32),
            pltpu.VMEM((2 * cols, TILE), F32),
            pltpu.VMEM((n_tiles, cols, TILE), BF16),
            pltpu.VMEM((n_tiles, cols, TILE), BF16),
            pltpu.VMEM((n_own, 8, cols), F32),
            pltpu.VMEM((n_sub, 8, cols), F32),
            pltpu.VMEM((n_grp, 8, cols), F32),
            pltpu.VMEM((n_own, 8, cols), F32),
            dma((2,)), dma((2,)),
            dma((1,)), dma((1,)),
            dma((n_grp,)), dma((n_grp,)),
            dma((1,)), dma((1,)),
            dma((n_tiles,)), dma((n_tiles,)),
            dma((1,)), dma((1,)),
            dma((n_grp,)), dma((n_grp,)),
            dma((1,)), dma((1,)),
            dma((4,)),
            pltpu.VMEM((cols, panels), BF16),
            dma((1,)),
        ],
        compiler_params=pltpu.CompilerParams(
            collective_id=0, has_side_effects=True, vmem_limit_bytes=56 << 20
        ),
    )(vectors, geometry, transfer, jnp.asarray(direction_table(dir_count)))
    return tuple(
        pl.pallas_call(
            factor_kernel,
            out_shape=(
                jax.ShapeDtypeStruct((cols, panels), F32),
                jax.ShapeDtypeStruct((cols, cols), F32),
            ),
            in_specs=[pl.BlockSpec(memory_space=pl.ANY)] * 2,
            out_specs=[pl.BlockSpec(memory_space=pltpu.VMEM)] * 2,
            scratch_shapes=[
                pltpu.VMEM((cols, cols), F32),
                pltpu.VMEM((cols, cols), F32),
                pltpu.VMEM((cols, panels), BF16),
                dma((2,)),
            ],
            compiler_params=pltpu.CompilerParams(vmem_limit_bytes=56 << 20),
        )(gram, applied)
    )


def solution(mesh):
    in_specs = (P(None, ("grp", "sub")), P(None, ("grp", "sub")), P(None, "grp", None, None))
    out_specs = (P(None, ("grp", "sub")), P())
    body = functools.partial(shards, mesh.shape["grp"], mesh.shape["sub"])
    return jax.shard_map(body, mesh=mesh, in_specs=in_specs, out_specs=out_specs, check_vma=False)
```
